32 devices in a mesh: scene: 4 (over y, x), row: 4 (over z), col: 2 (over core).
Axes of the slice: x: 2, y: 2, z: 4, core: 2. Of those that a mesh axis runs over, the one named last changes fastest.
Arguments:
- scenes: bfloat16 [4, 256, 128, 128], P('scene', 'row', 'col'), may hold values from -6 to 6
- cotangent: bfloat16 [4, 256, 128, 128], P('scene', 'row', 'col'), may hold values from -0.016479492 to 0.016479492
- params: float32 [294912], P(('scene', 'row', 'col')), may hold values from -0.1875 to 0.1875
- partials: float32 [32, 294912], P(('scene', 'row', 'col')), may hold values from -8 to 8
Outputs:
- sam_grad: float32 [294912], P(('scene', 'row', 'col'))
The draws below stay inside these ranges and needn't reach their ends.
All inputs are finite; a program needn't handle non-finite values.
Results may differ from the reference program's by a relative error of at most 0.0042.
Values may be sent and summed in bfloat16 or wider, within the bound.
A program may use at most 64 MiB of HBM per device.

```python
import jax
import jax.numpy as jnp
from jax import lax

C = 128
SCENES = 4
HEIGHT = 256
WIDTH = 128
DEVICES = 32


def with_spikes(result, stream_key, source, target, parts, factor):
    owner, partner = [(jnp.arange(result.shape[position]) // (result.shape[position] // parts)).reshape([-1 if axis == position else 1 for axis in range(result.ndim)]) for position in (source, target)]
    chosen = jax.random.permutation(stream_key, parts)[partner]
    strong = (owner == chosen) | (owner == (partner + parts // 2) % parts)
    return jnp.where(strong, factor * result, result)


def steps_of(rng, extent, cuts, smallest, top_value):
    loudness, own = 1.0, jax.random.fold_in(rng, 6)
    for position, shards_of in cuts:
        draws = jnp.exp(jax.random.uniform(jax.random.fold_in(own, position), (shards_of,), jnp.float32, smallest / len(cuts), top_value / len(cuts)))
        loudness = loudness * jnp.repeat(draws, extent[position] // shards_of).reshape([-1 if axis == position else 1 for axis in range(len(extent))])
    return loudness


def bell_draw(own_key, shape, scale, limit, shards=(), dtype=jnp.bfloat16):
    drawn = scale * jax.random.normal(own_key, shape, jnp.float32)
    if shards:
        drawn = drawn * steps_of(own_key, shape, shards, -0.22, 0.18)
    return jnp.clip(drawn, -limit, limit).astype(dtype)


def noise_with(own_key, dims, scale, bound, cuts, heavy, held_as=jnp.bfloat16):
    result = scale * jax.random.normal(own_key, dims, jnp.float32)
    if cuts:
        result = result * steps_of(own_key, dims, cuts, -0.22, 0.18)
    return jnp.clip(with_spikes(result, jax.random.fold_in(own_key, 3), *heavy), -bound, bound).astype(held_as)


def setup_inputs(seed: int = 0) -> dict:
    key_of = jax.random.split(jax.random.key(seed), 5)
    return {
        "scenes": bell_draw(key_of[0], (SCENES, HEIGHT, WIDTH, C), 1.0, 6.0, ((0, 4), (1, 4), (2, 2))),
        "cotangent": bell_draw(key_of[1], (SCENES, HEIGHT, WIDTH, C), ((SCENES * HEIGHT * WIDTH) ** -0.5), 0.016479492, ((0, 4), (1, 4), (2, 2))),
        "params": bell_draw(key_of[2], (18 * C * C,), (9 * C) ** -0.5, 0.1875, ((0, 32),), jnp.float32),
        "partials": noise_with(key_of[3], (DEVICES, 18 * C * C), 1.0, 8.0, ((0, 32),), (0, 1, 32, 2.75), jnp.float32),
    }


radius = 2.0
epsilon = 1e-06

def convolve(padded, kernel):
    return lax.conv_general_dilated(padded, kernel, (1, 1), 'VALID', dimension_numbers=('NHWC', 'HWIO', 'NHWC'), preferred_element_type=jnp.float32)

def border(field):
    return jnp.pad(field, ((0, 0), (1, 1), (1, 1), (0, 0)))

def kernel_grad(padded, errors):
    height = errors.shape[1]
    width = errors.shape[2]
    rows_out = []
    for row_off in range(3):
        cols_out = []
        for col_off in range(3):
            window = padded[:, row_off:row_off + height, col_off:col_off + width, :].astype(jnp.float32)
            cols_out.append(jnp.einsum('nhwc,nhwd->cd', window, errors.astype(jnp.float32)))
        rows_out.append(jnp.stack(cols_out))
    return jnp.stack(rows_out)

def reference(scenes, cotangent, params, partials):
    grads = lax.optimization_barrier(jnp.sum(partials, axis=0))
    factor = radius / (jnp.sqrt(jnp.sum(grads * grads)) + epsilon)
    perturbed = (params + factor * grads).astype(jnp.bfloat16)
    kernels = perturbed.reshape(2, 3, 3, scenes.shape[3], scenes.shape[3])
    kernel_one = kernels[0]
    kernel_two = kernels[1]
    flipped = jnp.transpose(kernel_two[::-1, ::-1], (0, 1, 3, 2))

    def one_scene(pair):
        inputs = pair[0][None]
        errors = pair[1][None]
        padded_in = border(inputs)
        pre = convolve(padded_in, kernel_one)
        hidden = jax.nn.silu(pre).astype(jnp.bfloat16)
        back = convolve(border(errors), flipped)
        squash = jax.nn.sigmoid(pre)
        delta = (back * squash * (1.0 + pre * (1.0 - squash))).astype(jnp.bfloat16)
        grad_one = kernel_grad(padded_in, delta)
        grad_two = kernel_grad(border(hidden), errors)
        return jnp.stack([grad_one, grad_two])
    per_scene = lax.map(one_scene, (scenes, cotangent))
    return lax.optimization_barrier(jnp.sum(per_scene, axis=0)).reshape(-1)
```

```python
import functools

import jax
import jax.numpy as jnp
from jax import lax
from jax.experimental import pallas as pl
from jax.experimental.pallas import tpu as pltpu
from jax.sharding import PartitionSpec as P

radius = 2.0
epsilon = 1e-06
AXES = ("scene", "row", "col")
MESH = pl.DeviceIdType.MESH
LANES = 128


class Place:
    def __init__(self, sizes):
        self.scenes, self.rows, self.cols = sizes
        self.pairs = self.cols // 2
        self.n = self.scenes * self.rows * self.pairs
        self.col = col = lax.axis_index("col")
        self.scene = lax.axis_index("scene")
        self.half = lax.rem(col, 2)
        self.m = self.scenes * self.pairs
        self.doublings = (self.rows - 1).bit_length()
        self.row = lax.axis_index("row")
        self.plane = lax.axis_index("scene") * self.pairs + col // 2
        self.me = self.chip(self.plane, self.row)

    def chip(self, plane, row):
        return (plane // self.pairs * self.rows + row) * self.pairs + lax.rem(plane, self.pairs)

    def plane_after(self, u):
        return lax.rem(self.plane + 1 + u, self.m)

    def row_after(self, t):
        return lax.rem(self.row + 1 + t, self.rows)

    def order(self, j):
        return self.chip(self.plane_after(lax.rem(j, self.m)), self.row_after(j // self.m))

    def device(self, chip, half):
        return {
            "scene": chip // (self.rows * self.pairs),
            "row": lax.rem(chip // self.pairs, self.rows),
            "col": lax.rem(chip, self.pairs) * 2 + half,
        }

    def beside(self, dr, dc):
        return {"scene": self.scene, "row": self.row + dr, "col": self.col + dc}

    def row_across(self, step):
        span = 2**step
        return self.row + span - 2 * span * lax.rem(self.row // span, 2)

    def plane_before(self, u):
        return lax.rem(self.plane + 2 * self.m - 1 - u, self.m)


def loop(low, high, body, unroll=1):
    def wrapped(j, carry):
        body(j)
        return carry

    lax.fori_loop(low, high, wrapped, 0, unroll=unroll)


def wait_all(ref, sem):
    pltpu.make_async_copy(ref, ref, sem).wait()


def inside(place, dr, dc):
    row, col = place.row + dr, place.col + dc
    fits = jnp.logical_and(row >= 0, row < place.rows)
    return jnp.logical_and(fits, jnp.logical_and(col >= 0, col < place.cols))


def greet(place):
    barrier = pltpu.get_barrier_semaphore()

    def signal(device):
        pl.semaphore_signal(barrier, inc=1, device_id=device, device_id_type=MESH)

    signal(place.device(place.me, 1 - place.half))
    for dr in (-1, 1):
        for dc in (-1, 1):

            @pl.when(inside(place, dr, dc))
            def _():
                signal(place.beside(dr, dc))

    def plane_peer(u):
        chip = place.chip(place.plane_after(u), place.row)
        signal(place.device(chip, place.half))
        signal(place.device(chip, 1 - place.half))

    loop(0, place.m - 1, plane_peer)
    def row_peer(t):
        signal(place.device(place.chip(place.plane, place.row_after(t)), place.half))

    loop(0, place.rows - 1, row_peer)
    expected = jnp.int32(2 * place.m - 1 + place.rows - 1)
    for dr in (-1, 1):
        for dc in (-1, 1):
            expected = expected + inside(place, dr, dc).astype(jnp.int32)
    return barrier, expected


AROUND = tuple((dr, dc) for dr in (-1, 0, 1) for dc in (-1, 0, 1) if dr or dc)


def edge_of(dr, dc):
    if dr:
        return 1 if dr < 0 else 0
    return 3 if dc < 0 else 2


def halo_copies(place, edges, halo, halo_send, halo_recv):
    copies = []
    for slot, (dr, dc) in enumerate(AROUND):
        src, dst = edges.at[edge_of(dr, dc)], halo.at[slot]
        if dr and dc:
            width = edges.shape[2]
            part = pl.ds(width - 16, 16) if dc < 0 else pl.ds(0, 16)
            src, dst = src.at[:, part], dst.at[:, part]
        copy = pltpu.make_async_remote_copy(
            src_ref=src,
            dst_ref=dst,
            send_sem=halo_send.at[slot],
            recv_sem=halo_recv.at[slot],
            device_id=place.beside(-dr, -dc),
            device_id_type=MESH,
        )
        copies.append((copy, inside(place, -dr, -dc), inside(place, dr, dc)))
    return copies


def fill(place, which, cells, halo, cat, cols):
    height, width, channels = cells.shape

    def arrived(dr, dc):
        block = halo[AROUND.index((dr, dc)), which].astype(jnp.float32)
        return jnp.where(inside(place, dr, dc), block, 0.0)

    position = lax.broadcasted_iota(jnp.int32, (width, channels), 0)

    def put(r, line, left, right):
        before = jnp.where(position == 0, left, pltpu.roll(line, 1, 0))
        behind = jnp.where(position == width - 1, right, pltpu.roll(line, width - 1, 0))
        cat[r, :, 0:channels] = before.astype(cat.dtype)
        cat[r, :, channels : 2 * channels] = line.astype(cat.dtype)
        cat[r, :, 2 * channels : 3 * channels] = behind.astype(cat.dtype)

    cols[0] = arrived(0, -1)
    cols[1] = arrived(0, 1)
    for dr, r in ((-1, 0), (1, height + 1)):
        put(r, arrived(dr, 0), arrived(dr, -1)[width - 1 : width], arrived(dr, 1)[0:1])

    def inner(r):
        put(r + 1, cells[r].astype(jnp.float32), cols[0, pl.ds(r, 1), :], cols[1, pl.ds(r, 1), :])

    loop(0, height, inner, unroll=4)


def row_pairs(cat, layer, start, pairs):
    width, channels = cat.shape[2:]
    return jnp.concatenate(
        [jnp.concatenate([cat[layer, start + 2 * p + a] for p in range(pairs)], axis=0) for a in range(4)], axis=1
    )


def kernel(sizes, block_rows, active_rows, data, params, scenes_hbm, cotangent_hbm, out,
           scenes, cotangent, edges, halo, cat, cols, flat, weights, outs, across, local,
           own, square, squares,
           theirs, sums, landed, kept, run, line_in, line_out,
           whole_own, whole_other, params_line,
           theirs_b, sums_b, landed_b, kept_b, passed_b, reached_b,
           load_sem, own_sem, halo_send, halo_recv,
           swap_send, swap_recv, plane_send, plane_recv, line_send, line_recv,
           sq_send, sq_recv, gather_send, gather_recv, relay_send, relay_recv,
           pass_send, pass_recv,
           swap_send_b, swap_recv_b, plane_send_b, plane_recv_b, row_send_b, row_recv_b):
    place = Place(sizes)
    n, m, lines, me, half = place.n, place.m, place.rows, place.me, place.half
    height, width, channels = scenes.shape
    rows = params.shape[0]
    taps = 9
    full, half_type = jnp.float32, jnp.bfloat16
    partner = place.device(me, 1 - half)

    def remote(src, dst, send_sem, recv_sem, device):
        return pltpu.make_async_remote_copy(
            src_ref=src, dst_ref=dst, send_sem=send_sem, recv_sem=recv_sem,
            device_id=device, device_id_type=MESH,
        )

    def plane_device(u, to_half):
        return place.device(place.chip(place.plane_after(u), place.row), to_half)

    loads = [
        pltpu.make_async_copy(scenes_hbm, scenes, load_sem.at[0]),
        pltpu.make_async_copy(cotangent_hbm, cotangent, load_sem.at[1]),
    ]

    def load_own(j):
        chip = place.chip(place.plane_after(lax.rem(j, m)), j // m)
        return pltpu.make_async_copy(data.at[chip, half], own.at[chip], own_sem.at[j])

    barrier, expected = greet(place)
    loop(0, n, lambda j: load_own(j).start())
    for load in loads:
        load.start()
    params_line[place.row] = params[...]
    for layer in range(2):
        weights[layer, 9 * channels : 12 * channels, 0:channels] = jnp.zeros((3 * channels, channels), half_type)
        weights[layer, 0 : 3 * channels, channels : 2 * channels] = jnp.zeros((3 * channels, channels), half_type)
    pl.semaphore_wait(barrier, expected)

    def swap(j):
        chip = place.chip(place.plane_after(lax.rem(j, m)), j // m)
        return remote(data.at[chip, 1 - half], theirs.at[chip], swap_send, swap_recv.at[j], partner)

    loop(0, n, lambda j: swap(j).start())

    def row_device(step):
        return place.device(place.chip(place.plane, place.row_across(step)), half)

    def passing(t):
        mine = params_line.at[place.row]
        chip = place.chip(place.plane, place.row_after(t))
        return remote(mine, mine, pass_send, pass_recv, place.device(chip, half))

    loop(0, lines - 1, lambda t: passing(t).start())

    def both(j):
        chip = place.chip(place.plane_after(lax.rem(j, m)), j // m)
        load_own(j).wait()
        swap(j).wait_recv()
        return own[chip] + theirs[chip]

    def across_plane(t):
        def pass_on(u):
            slot = t * (m - 1) + u
            sums[slot] = both(t * m + u).astype(sums.dtype)
            remote(sums.at[slot], landed.at[t, u], plane_send, plane_recv.at[t], plane_device(u, half)).start()

        loop(0, m - 1, pass_on)
        kept[t] = both(t * m + m - 1)

    loop(0, lines, across_plane)

    for which, (load, cells) in enumerate(zip(loads, (scenes, cotangent))):
        load.wait()
        edges[0, which] = cells[0]
        edges[1, which] = cells[height - 1]
        edges[2, which] = cells[:, 0:16, :].astype(full)[:, 0, :].astype(edges.dtype)
        edges[3, which] = cells[:, width - 16 : width, :].astype(full)[:, 15, :].astype(edges.dtype)
    halos = halo_copies(place, edges, halo, halo_send, halo_recv)
    for copy, out_of, into in halos:
        pl.when(out_of)(copy.start)

    def along(step, t):
        return remote(line_out.at[step, t], line_in.at[step, t], line_send.at[step, t], line_recv.at[step, t], row_device(step))

    def share(step, t, total):
        run[t] = total
        if step < place.doublings:
            line_out[step, t] = total.astype(half_type)
            along(step, t).start()

    def plane_sum(t):
        wait_all(landed.at[t], plane_recv.at[t])
        share(0, t, lax.fori_loop(0, m - 1, lambda u, sofar: sofar + landed[t, u].astype(full), kept[t]))

    def line_sum(step, t):
        along(step, t).wait_recv()
        share(step + 1, t, run[t] + line_in[step, t].astype(full))

    def first_sums(t):
        plane_sum(t)
        pl.when(t > 0)(lambda: line_sum(0, t - 1))

    if place.doublings:
        loop(0, lines, first_sums)
        line_sum(0, lines - 1)
    else:
        loop(0, lines, plane_sum)
    for copy, out_of, into in halos:
        pl.when(into)(copy.wait_recv)
    fill(place, 0, scenes, halo, cat.at[0], cols)
    for step in range(1, place.doublings):
        loop(0, lines, functools.partial(line_sum, step))
    square[0] = jnp.sum(lax.fori_loop(0, lines, lambda t, sofar: sofar + run[t] * run[t], jnp.zeros((rows, LANES), full)), axis=0, keepdims=True)

    def tell(device, slot):
        return remote(square.at[0], squares.at[slot], sq_send, sq_recv, device)

    def tell_chip(u):
        tell(plane_device(u, half), 2 * u + 1).start()
        tell(plane_device(u, 1 - half), 2 * u + 2).start()

    loop(0, m - 1, tell_chip)
    tell(partner, 0).start()
    fill(place, 1, cotangent, halo, cat.at[1], cols)
    wait_all(squares, sq_recv)
    norm2 = jnp.sum(square[0] + jnp.sum(squares[...], axis=0))
    factor = radius / (jnp.sqrt(jnp.full((1, LANES), norm2, full)) + epsilon)

    side = me // (n // 2)
    near_count = m // 2

    def towards(k, sign):
        near = side * near_count + lax.rem(place.plane + near_count * 2 + sign * (k + 1), near_count)
        far = (1 - side) * near_count + lax.rem(place.plane + near_count * 2 + sign * k, near_count)
        return near, far

    def give(plane, slot, t):
        mine = whole_own.at[t, place.plane]
        device = place.device(place.chip(plane, place.row), half)
        return remote(mine, mine, gather_send, gather_recv.at[t, slot], device)

    def relay(t, plane, far):
        return remote(whole_own.at[t, plane], whole_other.at[t, plane], relay_send, relay_recv.at[far], partner)

    wait_all(params_line.at[pl.ds(0, lines - 1)], pass_recv)

    def perturb(t):
        whole_own[t, place.plane] = (params_line[t] + factor * run[t]).astype(half_type)
        loop(0, near_count - 1, lambda k: give(towards(k, 1)[0], k, t).start())
        relay(t, place.plane, 0).start()

    loop(0, lines, perturb)

    def give_far(i):
        t, k = i // near_count, lax.rem(i, near_count)
        give(towards(k, 1)[1], near_count - 1 + k, t).start()

    loop(0, lines * near_count, give_far)

    def arrive(t, plane, slot, far):
        there = whole_own.at[t, plane]
        remote(there, there, gather_send, gather_recv.at[t, slot], partner).wait_recv()
        relay(t, plane, far).start()

    def from_near(i):
        t, k = i // (near_count - 1), lax.rem(i, near_count - 1)
        arrive(t, towards(k, -1)[0], k, 0)

    def from_far(i):
        t, k = i // near_count, lax.rem(i, near_count)
        arrive(t, towards(k, -1)[1], near_count - 1 + k, 1)

    def spread(layer, i):
        t, plane = i // near_count, layer * near_count + lax.rem(i, near_count)
        c = 2 * place.chip(plane, t)
        flat[pl.ds((c + half) * rows, rows), :] = whole_own[t, plane].astype(full)
        flat[pl.ds((c + 1 - half) * rows, rows), :] = whole_other[t, plane].astype(full)

    def put(layer, t, kernel):
        weights[layer, t * channels : (t + 1) * channels, 0:channels] = kernel
        weights[layer, (t + 3) * channels : (t + 4) * channels, channels : 2 * channels] = kernel

    def weigh(layer):
        wait_all(whole_other.at[:, pl.ds(0, near_count)], relay_recv.at[jnp.where(layer == side, 0, 1)])
        loop(0, lines * near_count, functools.partial(spread, layer), unroll=4)

        @pl.when(layer == 0)
        def _():
            for t in range(taps):
                put(0, t, flat[t * channels : (t + 1) * channels].astype(half_type))

        @pl.when(layer == 1)
        def _():
            for t in range(taps):
                first = (2 * taps - 1 - t) * channels
                put(1, t, flat[first : first + channels].T.astype(half_type))

    def convolve(layer, i):
        start = i * block_rows
        pairs = block_rows // 2
        pair = jnp.dot(row_pairs(cat, layer, start, pairs), weights[layer], preferred_element_type=full)
        for p in range(pairs):
            part = pair[p * width : (p + 1) * width]
            outs[layer, start + 2 * p] = part[:, 0:channels]
            outs[layer, start + 2 * p + 1] = part[:, channels:]

    def activate(i):
        block = pl.ds(i * active_rows, active_rows)
        cells = active_rows * width
        pre = outs[0, block].reshape(cells, channels)
        back = outs[1, block].reshape(cells, channels)
        squash = jax.nn.sigmoid(pre)
        at = pl.ds(pl.multiple_of(i * cells, cells), cells)
        across[0, :, at] = (back * squash * (1.0 + pre * (1.0 - squash))).T.astype(half_type)
        across[1, :, at] = (pre * squash).T.astype(half_type)

    loop(0, lines * (near_count - 1), from_near)
    weigh(side)
    loop(0, height // block_rows, functools.partial(convolve, side))
    loop(0, lines * near_count, from_far)
    weigh(1 - side)
    loop(0, height // block_rows, functools.partial(convolve, 1 - side))
    loop(0, height // active_rows, activate)

    def field_grad(a, low, high):
        first, last = 3 * a + low, 3 * a + high
        for layer in range(2):
            field = cat[layer, a : a + height, :, low * channels : high * channels].reshape(height * width, -1)
            grad = jnp.dot(across[layer], field, preferred_element_type=full)
            for t in range(first, last):
                tap = grad[:, (t - first) * channels : (t - first + 1) * channels]
                if layer == 0:
                    flat[t * channels : (t + 1) * channels] = tap.T
                else:
                    u = 2 * taps - 1 - t
                    flat[u * channels : (u + 1) * channels] = tap

    def swap_b(c):
        return remote(local.at[c, 1 - half], theirs_b.at[c], swap_send_b, swap_recv_b.at[c], partner)

    def ready(c):
        for h in range(2):
            local[c, h] = flat[pl.ds((2 * c + h) * rows, rows), :]
        swap_b(c).start()

    def pass_b(c):
        plane = c // (lines * place.pairs) * place.pairs + lax.rem(c, place.pairs)
        row = lax.rem(c // place.pairs, lines)
        swap_b(c).wait_recv()
        total = local[c, half] + theirs_b[c]

        @pl.when(plane == place.plane)
        def _():
            kept_b[row] = total

        @pl.when(plane != place.plane)
        def _():
            u = lax.rem(plane - place.plane - 1 + m, m)
            sums_b[c] = total.astype(half_type)
            remote(sums_b.at[c], landed_b.at[row, u], plane_send_b, plane_recv_b.at[row], plane_device(u, half)).start()

    def outermost(low, high, body):
        def each(j):
            body(j)
            body(n - 1 - j)

        loop(low, high, each)

    done = before = 0
    for a, low, high in ((0, 0, 3), (1, 0, 3), (2, 0, 2), (2, 2, 3)):
        field_grad(a, low, high)
        outermost(before, done, pass_b)
        before = done
        done = min((3 * a + high) * channels // (2 * rows), n // 2)
        outermost(before, done, ready)
    outermost(before, done, pass_b)

    def along_rows(k):
        row = jnp.where(side == 0, k, lines - 1 - k)
        wait_all(landed_b.at[row], plane_recv_b.at[row])
        total = lax.fori_loop(0, m - 1, lambda u, sofar: sofar + landed_b[row, u].astype(full), kept_b[row])
        kept_b[row] = total

        @pl.when(row != place.row)
        def _():
            t = lax.rem(row - place.row - 1 + lines, lines)
            passed_b[t] = total.astype(half_type)
            device = place.device(place.chip(place.plane, row), half)
            remote(passed_b.at[t], reached_b.at[t], row_send_b, row_recv_b, device).start()

    loop(0, lines, along_rows)
    wait_all(theirs, swap_send)
    wait_all(sums, plane_send)
    wait_all(squares, sq_send)
    wait_all(whole_other, relay_send)
    wait_all(params_line.at[pl.ds(0, lines - 1)], pass_send)
    wait_all(whole_own.at[:, pl.ds(0, m - 1)], gather_send)
    for copy, out_of, into in halos:
        pl.when(out_of)(copy.wait_send)
    for step in range(place.doublings):
        loop(0, lines, lambda t: along(step, t).wait_send())
    wait_all(theirs_b, swap_send_b)
    wait_all(sums_b.at[pl.ds(0, n - lines)], plane_send_b)
    wait_all(reached_b, row_recv_b)
    out[...] = lax.fori_loop(0, lines - 1, lambda t, sofar: sofar + reached_b[t].astype(full), kept_b[place.row])
    wait_all(reached_b, row_send_b)


def on_device(sizes, scenes, cotangent, params, partials):
    scenes, cotangent = scenes[0], cotangent[0]
    height, width, channels = scenes.shape
    n = sizes[0] * sizes[1] * sizes[2] // 2
    rows = params.size // LANES
    dma = pltpu.SemaphoreType.DMA
    half_type, full = jnp.bfloat16, jnp.float32
    anywhere, vmem = pl.BlockSpec(memory_space=pl.ANY), pl.BlockSpec(memory_space=pltpu.VMEM)
    lines, m = sizes[1], n // sizes[1]
    one = (rows, LANES)
    doublings = max((lines - 1).bit_length(), 1)
    scratch = [
        pltpu.VMEM(scenes.shape, half_type),
        pltpu.VMEM(scenes.shape, half_type),
        pltpu.VMEM((4, 2, width, channels), half_type),
        pltpu.VMEM((len(AROUND), 2, width, channels), half_type),
        pltpu.VMEM((2, height + 2, width, 3 * channels), half_type),
        pltpu.VMEM((2, height, channels), full),
        pltpu.VMEM((18 * channels, channels), full),
        pltpu.VMEM((2, 12 * channels, 2 * channels), half_type),
        pltpu.VMEM((2, height, width, channels), full),
        pltpu.VMEM((2, channels, height * width), half_type),
        pltpu.VMEM((n, 2, *one), full),
        pltpu.VMEM((n, *one), full),
        pltpu.VMEM((1, 1, LANES), full),
        pltpu.VMEM((2 * m - 1, 1, LANES), full),
        pltpu.VMEM((n, *one), full),
        pltpu.VMEM((n - lines, *one), half_type),
        pltpu.VMEM((lines, m - 1, *one), half_type),
        pltpu.VMEM((lines, *one), full),
        pltpu.VMEM((lines, *one), full),
        pltpu.VMEM((doublings, lines, *one), half_type),
        pltpu.VMEM((doublings, lines, *one), half_type),
        pltpu.VMEM((lines, m, *one), half_type),
        pltpu.VMEM((lines, m, *one), half_type),
        pltpu.VMEM((lines, *one), full),
        pltpu.VMEM((n, *one), full),
        pltpu.VMEM((n, *one), half_type),
        pltpu.VMEM((lines, m - 1, *one), half_type),
        pltpu.VMEM((lines, *one), full),
        pltpu.VMEM((lines - 1, *one), half_type),
        pltpu.VMEM((lines - 1, *one), half_type),
        dma((2,)), dma((n,)), dma((len(AROUND),)), dma((len(AROUND),)),
        dma, dma((n,)), dma, dma((lines,)), dma((doublings, lines)), dma((doublings, lines)),
        dma, dma, dma, dma((lines, m - 1)), dma, dma((2,)),
        dma, dma,
        dma, dma((n,)), dma, dma((lines,)), dma, dma,
    ]
    grads = pl.pallas_call(
        functools.partial(kernel, sizes, 32, 16),
        out_shape=jax.ShapeDtypeStruct((rows, LANES), full),
        in_specs=[anywhere, vmem, anywhere, anywhere],
        out_specs=vmem,
        scratch_shapes=scratch,
        compiler_params=pltpu.CompilerParams(
            collective_id=0, has_side_effects=True, vmem_limit_bytes=56 * 2**20
        ),
        name="sam_grad",
    )(partials[0].reshape(n, 2, rows, LANES), params.reshape(rows, LANES), scenes, cotangent)
    return grads.reshape(-1)


def solution(mesh):
    sizes = tuple(mesh.shape[axis] for axis in AXES)
    return jax.shard_map(
        functools.partial(on_device, sizes),
        mesh=mesh,
        in_specs=(
            P("scene", "row", "col", None),
            P("scene", "row", "col", None),
            P(AXES),
            P(AXES, None),
        ),
        out_specs=P(AXES),
        check_vma=False,
    )
```

```python
import functools

import jax
import jax.numpy as jnp
from jax import lax
from jax.experimental import pallas as pl
from jax.experimental.pallas import tpu as pltpu
from jax.sharding import PartitionSpec as P

radius = 2.0
epsilon = 1e-06
AXES = ("scene", "row", "col")
MESH = pl.DeviceIdType.MESH
LANES = 128
TAP_GROUPS = ((0, 1, 4, 5), (2, 6), (3, 7), (8,))


class Place:
    def __init__(self, sizes):
        self.scenes, self.rows, self.cols = sizes
        self.pairs = self.cols // 2
        self.n = self.scenes * self.rows * self.pairs
        self.col = col = lax.axis_index("col")
        self.scene = lax.axis_index("scene")
        self.half = lax.rem(col, 2)
        self.m = self.scenes * self.pairs
        self.doublings = (self.rows - 1).bit_length()
        self.row = lax.axis_index("row")
        self.plane = lax.axis_index("scene") * self.pairs + col // 2
        self.me = self.chip(self.plane, self.row)

    def chip(self, plane, row):
        return (plane // self.pairs * self.rows + row) * self.pairs + lax.rem(plane, self.pairs)

    def plane_after(self, u):
        return lax.rem(self.plane + 1 + u, self.m)

    def row_after(self, t):
        return lax.rem(self.row + 1 + t, self.rows)

    def order(self, j):
        return self.chip(self.plane_after(lax.rem(j, self.m)), self.row_after(j // self.m))

    def device(self, chip, half):
        return {
            "scene": chip // (self.rows * self.pairs),
            "row": lax.rem(chip // self.pairs, self.rows),
            "col": lax.rem(chip, self.pairs) * 2 + half,
        }

    def beside(self, dr, dc):
        return {"scene": self.scene, "row": self.row + dr, "col": self.col + dc}

    def row_across(self, step):
        span = 2**step
        return self.row + span - 2 * span * lax.rem(self.row // span, 2)

    def plane_before(self, u):
        return lax.rem(self.plane + 2 * self.m - 1 - u, self.m)


def loop(low, high, body, unroll=1):
    def wrapped(j, carry):
        body(j)
        return carry

    lax.fori_loop(low, high, wrapped, 0, unroll=unroll)


def wait_all(ref, sem):
    pltpu.make_async_copy(ref, ref, sem).wait()


def inside(place, dr, dc):
    row, col = place.row + dr, place.col + dc
    fits = jnp.logical_and(row >= 0, row < place.rows)
    return jnp.logical_and(fits, jnp.logical_and(col >= 0, col < place.cols))


def greeted(place, dr, dc):
    if dc:
        return inside(place, dr, dc)
    first = place.row_across(0) if place.doublings else place.row
    return jnp.logical_and(inside(place, dr, dc), first != place.row + dr)


def greet(place):
    barrier = pltpu.get_barrier_semaphore()

    def signal(device):
        pl.semaphore_signal(barrier, inc=1, device_id=device, device_id_type=MESH)

    signal(place.device(place.me, 1 - place.half))
    for dr in (-1, 1):
        for dc in (-1, 0, 1):

            @pl.when(greeted(place, dr, dc))
            def _():
                signal(place.beside(dr, dc))

    def plane_peer(u):
        chip = place.chip(place.plane_after(u), place.row)
        signal(place.device(chip, place.half))
        signal(place.device(chip, 1 - place.half))

    loop(0, place.m - 1, plane_peer)
    for step in range(place.doublings):
        signal(place.device(place.chip(place.plane, place.row_across(step)), place.half))
    expected = jnp.int32(2 * place.m - 1 + place.doublings)
    for dr in (-1, 1):
        for dc in (-1, 0, 1):
            expected = expected + greeted(place, dr, dc).astype(jnp.int32)
    return barrier, expected


AROUND = tuple((dr, dc) for dr in (-1, 0, 1) for dc in (-1, 0, 1) if dr or dc)


def edge_of(dr, dc):
    if dr:
        return 1 if dr < 0 else 0
    return 3 if dc < 0 else 2


def halo_copies(place, edges, halo, halo_send, halo_recv):
    copies = []
    for slot, (dr, dc) in enumerate(AROUND):
        src, dst = edges.at[edge_of(dr, dc)], halo.at[slot]
        if dr and dc:
            width = edges.shape[2]
            part = pl.ds(width - 16, 16) if dc < 0 else pl.ds(0, 16)
            src, dst = src.at[:, part], dst.at[:, part]
        copy = pltpu.make_async_remote_copy(
            src_ref=src,
            dst_ref=dst,
            send_sem=halo_send.at[slot],
            recv_sem=halo_recv.at[slot],
            device_id=place.beside(-dr, -dc),
            device_id_type=MESH,
        )
        copies.append((copy, inside(place, -dr, -dc), inside(place, dr, dc)))
    return copies


def fill(place, which, cells, halo, cat, cols):
    height, width, channels = cells.shape

    def arrived(dr, dc):
        block = halo[AROUND.index((dr, dc)), which].astype(jnp.float32)
        return jnp.where(inside(place, dr, dc), block, 0.0)

    position = lax.broadcasted_iota(jnp.int32, (width, channels), 0)

    def put(r, line, left, right):
        before = jnp.where(position == 0, left, pltpu.roll(line, 1, 0))
        behind = jnp.where(position == width - 1, right, pltpu.roll(line, width - 1, 0))
        cat[r, :, 0:channels] = before.astype(cat.dtype)
        cat[r, :, channels : 2 * channels] = line.astype(cat.dtype)
        cat[r, :, 2 * channels : 3 * channels] = behind.astype(cat.dtype)

    cols[0] = arrived(0, -1)
    cols[1] = arrived(0, 1)
    for dr, r in ((-1, 0), (1, height + 1)):
        put(r, arrived(dr, 0), arrived(dr, -1)[width - 1 : width], arrived(dr, 1)[0:1])

    def inner(r):
        put(r + 1, cells[r].astype(jnp.float32), cols[0, pl.ds(r, 1), :], cols[1, pl.ds(r, 1), :])

    loop(0, height, inner, unroll=4)


def row_pairs(cat, layer, start, pairs):
    width, channels = cat.shape[2:]
    return jnp.concatenate(
        [jnp.concatenate([cat[layer, start + 2 * p + a] for p in range(pairs)], axis=0) for a in range(4)], axis=1
    )


def kernel(sizes, block_rows, data, params, scenes_hbm, cotangent_hbm, out,
           scenes, cotangent, edges, halo, cat, cols, flat, weights, outs, across, local,
           own, square, squares,
           theirs, sums, landed, kept, run, line_in, line_out,
           whole_own, whole_other, params_line,
           theirs_b, sums_b, landed_b, kept_b, passed_b, reached_b,
           load_sem, own_sem, halo_send, halo_recv,
           swap_send, swap_recv, plane_send, plane_recv, line_send, line_recv,
           sq_send, sq_recv, gather_send, gather_recv, relay_send, relay_recv,
           pass_send, pass_recv,
           swap_send_b, swap_recv_b, plane_send_b, plane_recv_b, row_send_b, row_recv_b):
    place = Place(sizes)
    n, m, lines, me, half = place.n, place.m, place.rows, place.me, place.half
    height, width, channels = scenes.shape
    rows = params.shape[0]
    taps = 9
    full, half_type = jnp.float32, jnp.bfloat16
    partner = place.device(me, 1 - half)

    def remote(src, dst, send_sem, recv_sem, device):
        return pltpu.make_async_remote_copy(
            src_ref=src, dst_ref=dst, send_sem=send_sem, recv_sem=recv_sem,
            device_id=device, device_id_type=MESH,
        )

    def plane_device(u, to_half):
        return place.device(place.chip(place.plane_after(u), place.row), to_half)

    loads = [
        pltpu.make_async_copy(scenes_hbm, scenes, load_sem.at[0]),
        pltpu.make_async_copy(cotangent_hbm, cotangent, load_sem.at[1]),
    ]

    def load_own(j):
        chip = place.chip(place.plane_after(lax.rem(j, m)), j // m)
        return pltpu.make_async_copy(data.at[chip, half], own.at[chip], own_sem.at[j])

    barrier, expected = greet(place)
    load_params = pltpu.make_async_copy(params, params_line.at[place.row], load_sem.at[2])
    load_params.start()
    loop(0, n, lambda j: load_own(j).start())
    for load in loads:
        load.start()
    for layer in range(2):
        weights[layer, 9 * channels : 12 * channels, 0:channels] = jnp.zeros((3 * channels, channels), half_type)
        weights[layer, 0 : 3 * channels, channels : 2 * channels] = jnp.zeros((3 * channels, channels), half_type)
    pl.semaphore_wait(barrier, expected)

    def swap(j):
        chip = place.chip(place.plane_after(lax.rem(j, m)), j // m)
        return remote(data.at[chip, 1 - half], theirs.at[chip], swap_send, swap_recv.at[j], partner)

    loop(0, n, lambda j: swap(j).start())

    def row_device(step):
        return place.device(place.chip(place.plane, place.row_across(step)), half)

    def passing(step, row):
        block = params_line.at[row]
        return remote(block, block, pass_send, pass_recv.at[step], row_device(step))

    load_params.wait()
    for step in range(place.doublings):
        passing(step, place.row).start()

    def others(step):
        span = 2**step
        first = place.row // span * span
        return [first + lax.rem(place.row - first + k, span) for k in range(1, span)]

    def pass_on_params(step):
        for row in others(step):
            passing(step, row).start()

    def params_come(step):
        wait_all(params_line.at[pl.ds(0, 2**step)], pass_recv.at[step])

    def both(j):
        chip = place.chip(place.plane_after(lax.rem(j, m)), j // m)
        load_own(j).wait()
        swap(j).wait_recv()
        return own[chip] + theirs[chip]

    def across_plane(t):
        def pass_on(u):
            slot = t * (m - 1) + u
            sums[slot] = both(t * m + u).astype(sums.dtype)
            remote(sums.at[slot], landed.at[t, u], plane_send, plane_recv.at[t], plane_device(u, half)).start()

        loop(0, m - 1, pass_on)
        kept[t] = both(t * m + m - 1)

    loop(0, lines, across_plane)

    for which, (load, cells) in enumerate(zip(loads, (scenes, cotangent))):
        load.wait()
        edges[0, which] = cells[0]
        edges[1, which] = cells[height - 1]
        edges[2, which] = cells[:, 0:16, :].astype(full)[:, 0, :].astype(edges.dtype)
        edges[3, which] = cells[:, width - 16 : width, :].astype(full)[:, 15, :].astype(edges.dtype)
    halos = halo_copies(place, edges, halo, halo_send, halo_recv)
    for copy, out_of, into in halos:
        pl.when(out_of)(copy.start)

    def along(step, t):
        return remote(line_out.at[step, t], line_in.at[step, t], line_send.at[step, t], line_recv.at[step, t], row_device(step))

    def share(step, t, total):
        run[t] = total
        if step < place.doublings:
            line_out[step, t] = total.astype(half_type)
            along(step, t).start()

    def plane_sum(t):
        wait_all(landed.at[t], plane_recv.at[t])
        share(0, t, lax.fori_loop(0, m - 1, lambda u, sofar: sofar + landed[t, u].astype(full), kept[t]))

    def line_sum(step, t):
        along(step, t).wait_recv()
        share(step + 1, t, run[t] + line_in[step, t].astype(full))

    if place.doublings > 1:
        params_come(0)
        pass_on_params(1)
    loop(0, lines, plane_sum)
    if place.doublings:
        loop(0, lines, functools.partial(line_sum, 0))
    for step in range(2, place.doublings):
        params_come(step - 1)
        pass_on_params(step)
    for copy, out_of, into in halos:
        pl.when(into)(copy.wait_recv)
    fill(place, 0, scenes, halo, cat.at[0], cols)
    for step in range(1, place.doublings):
        loop(0, lines, functools.partial(line_sum, step))
    square[0] = jnp.sum(lax.fori_loop(0, lines, lambda t, sofar: sofar + run[t] * run[t], jnp.zeros((rows, LANES), full)), axis=0, keepdims=True)

    def tell(device, slot):
        return remote(square.at[0], squares.at[slot], sq_send, sq_recv, device)

    def tell_chip(u):
        tell(plane_device(u, half), 2 * u + 1).start()
        tell(plane_device(u, 1 - half), 2 * u + 2).start()

    loop(0, m - 1, tell_chip)
    tell(partner, 0).start()
    fill(place, 1, cotangent, halo, cat.at[1], cols)
    wait_all(squares, sq_recv)
    norm2 = jnp.sum(square[0] + jnp.sum(squares[...], axis=0))
    factor = radius / (jnp.sqrt(jnp.full((1, LANES), norm2, full)) + epsilon)

    side = me // (n // 2)
    near_count = m // 2

    def towards(k, sign):
        near = side * near_count + lax.rem(place.plane + near_count * 2 + sign * (k + 1), near_count)
        far = (1 - side) * near_count + lax.rem(place.plane + near_count * 2 + sign * k, near_count)
        return near, far

    def give(plane, slot, t):
        mine = whole_own.at[t, place.plane]
        device = place.device(place.chip(plane, place.row), half)
        return remote(mine, mine, gather_send, gather_recv.at[t, slot], device)

    def relay(t, plane, far):
        return remote(whole_own.at[t, plane], whole_other.at[t, plane], relay_send, relay_recv.at[far], partner)

    for step in range(max(place.doublings - 1, 0), place.doublings):
        params_come(step)

    def perturb(t):
        whole_own[t, place.plane] = (params_line[t] + factor * run[t]).astype(half_type)
        loop(0, near_count - 1, lambda k: give(towards(k, 1)[0], k, t).start())
        relay(t, place.plane, 0).start()

    loop(0, lines, perturb)

    def give_far(i):
        t, k = i // near_count, lax.rem(i, near_count)
        give(towards(k, 1)[1], near_count - 1 + k, t).start()

    loop(0, lines * near_count, give_far)

    def arrive(t, plane, slot, far):
        there = whole_own.at[t, plane]
        remote(there, there, gather_send, gather_recv.at[t, slot], partner).wait_recv()
        relay(t, plane, far).start()

    def from_near(i):
        t, k = i // (near_count - 1), lax.rem(i, near_count - 1)
        arrive(t, towards(k, -1)[0], k, 0)

    def from_far(i):
        t, k = i // near_count, lax.rem(i, near_count)
        arrive(t, towards(k, -1)[1], near_count - 1 + k, 1)

    def spread(layer, i):
        t, plane = i // near_count, layer * near_count + lax.rem(i, near_count)
        c = 2 * place.chip(plane, t)
        flat[pl.ds((c + half) * rows, rows), :] = whole_own[t, plane].astype(full)
        flat[pl.ds((c + 1 - half) * rows, rows), :] = whole_other[t, plane].astype(full)

    def put(layer, t, kernel):
        weights[layer, t * channels : (t + 1) * channels, 0:channels] = kernel
        weights[layer, (t + 3) * channels : (t + 4) * channels, channels : 2 * channels] = kernel

    def weigh(layer):
        wait_all(whole_other.at[:, pl.ds(0, near_count)], relay_recv.at[jnp.where(layer == side, 0, 1)])
        loop(0, lines * near_count, functools.partial(spread, layer), unroll=4)

        @pl.when(layer == 0)
        def _():
            for t in range(taps):
                put(0, t, flat[t * channels : (t + 1) * channels].astype(half_type))

        @pl.when(layer == 1)
        def _():
            for t in range(taps):
                first = (2 * taps - 1 - t) * channels
                put(1, t, flat[first : first + channels].T.astype(half_type))

    blocks, pairs = height // block_rows, block_rows // 2

    def convolve(layer, i):
        start = i * block_rows
        pair = jnp.dot(row_pairs(cat, layer, start, pairs), weights[layer], preferred_element_type=full)
        both_rows = []
        for p in range(pairs):
            part = pair[p * width : (p + 1) * width]
            both_rows.append(jnp.concatenate([part[:, 0:channels], part[:, channels:]], axis=0))
        return start, both_rows

    def convolve_near(i):
        start, both_rows = convolve(side, i)
        for p, cells in enumerate(both_rows):
            outs[pl.ds(start + 2 * p, 2)] = cells.reshape(2, width, channels)

    def convolve_far(i):
        start, both_rows = convolve(1 - side, i)
        for p, cells in enumerate(both_rows):
            near = outs[pl.ds(start + 2 * p, 2)].reshape(2 * width, channels)
            pre = jnp.where(side == 0, near, cells)
            back = jnp.where(side == 0, cells, near)
            squash = jax.nn.sigmoid(pre)
            at = pl.ds(pl.multiple_of((start + 2 * p) * width, 2 * width), 2 * width)
            across[0, :, at] = (back * squash * (1.0 + pre * (1.0 - squash))).T.astype(half_type)
            across[1, :, at] = (pre * squash).T.astype(half_type)

    loop(0, lines * (near_count - 1), from_near)
    weigh(side)
    def near_block(i):
        pl.when(i == blocks // 2)(lambda: loop(0, lines * near_count, from_far))
        convolve_near(i)

    loop(0, blocks, near_block)
    weigh(1 - side)
    loop(0, blocks, convolve_far)

    def field_grad(group):
        for layer in range(2):
            field = jnp.concatenate([
                cat[layer, u // 3 : u // 3 + height, :, u % 3 * channels : (u % 3 + 1) * channels].reshape(height * width, channels)
                for u in group
            ], axis=1)
            grad = jnp.dot(across[layer], field, preferred_element_type=full)
            for i, u in enumerate(group):
                tap = grad[:, i * channels : (i + 1) * channels]
                if layer == 0:
                    flat[u * channels : (u + 1) * channels] = tap.T
                else:
                    t = 2 * taps - 1 - u
                    flat[t * channels : (t + 1) * channels] = tap

    def swap_b(c):
        return remote(local.at[c, 1 - half], theirs_b.at[c], swap_send_b, swap_recv_b.at[c], partner)

    def ready(c):
        for h in range(2):
            local[c, h] = flat[pl.ds((2 * c + h) * rows, rows), :]
        swap_b(c).start()

    def pass_b(c):
        plane = c // (lines * place.pairs) * place.pairs + lax.rem(c, place.pairs)
        row = lax.rem(c // place.pairs, lines)
        swap_b(c).wait_recv()
        total = local[c, half] + theirs_b[c]

        @pl.when(plane == place.plane)
        def _():
            kept_b[row] = total

        @pl.when(plane != place.plane)
        def _():
            u = lax.rem(plane - place.plane - 1 + m, m)
            sums_b[c] = total.astype(half_type)
            remote(sums_b.at[c], landed_b.at[row, u], plane_send_b, plane_recv_b.at[row], plane_device(u, half)).start()

    def completed_by(c):
        touched = range(2 * c * rows // channels, (2 * (c + 1) * rows - 1) // channels + 1)
        return max(i for i, group in enumerate(TAP_GROUPS) if any(t in group for t in touched))

    def each_chunk(i, body):
        def mirrored(c):
            body(c)
            body(n - 1 - c)

        chunks = [c for c in range(n // 2) if completed_by(c) == i]
        starts = [c for c in chunks if c - 1 not in chunks]
        ends = [c + 1 for c in chunks if c + 1 not in chunks]
        for low, high in zip(starts, ends):
            loop(low, high, mirrored)

    for i, group in enumerate(TAP_GROUPS):
        field_grad(group)
        if i:
            each_chunk(i - 1, pass_b)
        each_chunk(i, ready)
    each_chunk(len(TAP_GROUPS) - 1, pass_b)

    def along_rows(k):
        row = jnp.where(side == 0, k, lines - 1 - k)
        wait_all(landed_b.at[row], plane_recv_b.at[row])
        total = lax.fori_loop(0, m - 1, lambda u, sofar: sofar + landed_b[row, u].astype(full), kept_b[row])
        kept_b[row] = total

        @pl.when(row != place.row)
        def _():
            t = lax.rem(row - place.row - 1 + lines, lines)
            passed_b[t] = total.astype(half_type)
            device = place.device(place.chip(place.plane, row), half)
            remote(passed_b.at[t], reached_b.at[t], row_send_b, row_recv_b, device).start()

    loop(0, lines, along_rows)
    wait_all(theirs, swap_send)
    wait_all(sums, plane_send)
    wait_all(squares, sq_send)
    wait_all(whole_other, relay_send)
    wait_all(params_line.at[pl.ds(0, lines - 1)], pass_send)
    wait_all(whole_own.at[:, pl.ds(0, m - 1)], gather_send)
    for copy, out_of, into in halos:
        pl.when(out_of)(copy.wait_send)
    for step in range(place.doublings):
        loop(0, lines, lambda t: along(step, t).wait_send())
    wait_all(theirs_b, swap_send_b)
    wait_all(sums_b.at[pl.ds(0, n - lines)], plane_send_b)
    wait_all(reached_b, row_recv_b)
    out[...] = lax.fori_loop(0, lines - 1, lambda t, sofar: sofar + reached_b[t].astype(full), kept_b[place.row])
    wait_all(reached_b, row_send_b)


def on_device(sizes, scenes, cotangent, params, partials):
    scenes, cotangent = scenes[0], cotangent[0]
    height, width, channels = scenes.shape
    n = sizes[0] * sizes[1] * sizes[2] // 2
    rows = params.size // LANES
    dma = pltpu.SemaphoreType.DMA
    half_type, full = jnp.bfloat16, jnp.float32
    anywhere, vmem = pl.BlockSpec(memory_space=pl.ANY), pl.BlockSpec(memory_space=pltpu.VMEM)
    lines, m = sizes[1], n // sizes[1]
    one = (rows, LANES)
    doublings = max((lines - 1).bit_length(), 1)
    scratch = [
        pltpu.VMEM(scenes.shape, half_type),
        pltpu.VMEM(scenes.shape, half_type),
        pltpu.VMEM((4, 2, width, channels), half_type),
        pltpu.VMEM((len(AROUND), 2, width, channels), half_type),
        pltpu.VMEM((2, height + 2, width, 3 * channels), half_type),
        pltpu.VMEM((2, height, channels), full),
        pltpu.VMEM((18 * channels, channels), full),
        pltpu.VMEM((2, 12 * channels, 2 * channels), half_type),
        pltpu.VMEM((height, width, channels), full),
        pltpu.VMEM((2, channels, height * width), half_type),
        pltpu.VMEM((n, 2, *one), full),
        pltpu.VMEM((n, *one), full),
        pltpu.VMEM((1, 1, LANES), full),
        pltpu.VMEM((2 * m - 1, 1, LANES), full),
        pltpu.VMEM((n, *one), full),
        pltpu.VMEM((n - lines, *one), half_type),
        pltpu.VMEM((lines, m - 1, *one), half_type),
        pltpu.VMEM((lines, *one), full),
        pltpu.VMEM((lines, *one), full),
        pltpu.VMEM((doublings, lines, *one), half_type),
        pltpu.VMEM((doublings, lines, *one), half_type),
        pltpu.VMEM((lines, m, *one), half_type),
        pltpu.VMEM((lines, m, *one), half_type),
        pltpu.VMEM((lines, *one), full),
        pltpu.VMEM((n, *one), full),
        pltpu.VMEM((n, *one), half_type),
        pltpu.VMEM((lines, m - 1, *one), half_type),
        pltpu.VMEM((lines, *one), full),
        pltpu.VMEM((lines - 1, *one), half_type),
        pltpu.VMEM((lines - 1, *one), half_type),
        dma((3,)), dma((n,)), dma((len(AROUND),)), dma((len(AROUND),)),
        dma, dma((n,)), dma, dma((lines,)), dma((doublings, lines)), dma((doublings, lines)),
        dma, dma, dma, dma((lines, m - 1)), dma, dma((2,)),
        dma, dma((doublings,)),
        dma, dma((n,)), dma, dma((lines,)), dma, dma,
    ]
    grads = pl.pallas_call(
        functools.partial(kernel, sizes, 32),
        out_shape=pltpu.VMEM((rows, LANES), full),
        in_specs=[anywhere, anywhere, anywhere, anywhere],
        out_specs=vmem,
        scratch_shapes=scratch,
        compiler_params=pltpu.CompilerParams(
            collective_id=0, has_side_effects=True, vmem_limit_bytes=56 * 2**20
        ),
        name="sam_grad",
    )(partials[0].reshape(n, 2, rows, LANES), params.reshape(rows, LANES), scenes, cotangent)
    return grads.reshape(-1)


def solution(mesh):
    sizes = tuple(mesh.shape[axis] for axis in AXES)
    return jax.shard_map(
        functools.partial(on_device, sizes),
        mesh=mesh,
        in_specs=(
            P("scene", "row", "col", None),
            P("scene", "row", "col", None),
            P(AXES),
            P(AXES, None),
        ),
        out_specs=P(AXES),
        check_vma=False,
    )
```

```python
import functools

import jax
import jax.numpy as jnp
from jax import lax
from jax.experimental import pallas as pl
from jax.experimental.pallas import tpu as pltpu
from jax.sharding import PartitionSpec as P

radius = 2.0
epsilon = 1e-06
AXES = ("scene", "row", "col")
MESH = pl.DeviceIdType.MESH
LANES = 128
TAP_GROUPS = ((0, 1, 4, 5), (2, 6), (3, 7), (8,))


class Place:
    def __init__(self, sizes):
        self.scenes, self.rows, self.cols = sizes
        self.pairs = self.cols // 2
        self.n = self.scenes * self.rows * self.pairs
        self.col = col = lax.axis_index("col")
        self.scene = lax.axis_index("scene")
        self.half = lax.rem(col, 2)
        self.m = self.scenes * self.pairs
        self.doublings = (self.rows - 1).bit_length()
        self.row = lax.axis_index("row")
        self.plane = lax.axis_index("scene") * self.pairs + col // 2
        self.me = self.chip(self.plane, self.row)

    def chip(self, plane, row):
        return (plane // self.pairs * self.rows + row) * self.pairs + lax.rem(plane, self.pairs)

    def plane_after(self, u):
        return lax.rem(self.plane + 1 + u, self.m)

    def row_after(self, t):
        return lax.rem(self.row + 1 + t, self.rows)

    def order(self, j):
        return self.chip(self.plane_after(lax.rem(j, self.m)), self.row_after(j // self.m))

    def device(self, chip, half):
        return {
            "scene": chip // (self.rows * self.pairs),
            "row": lax.rem(chip // self.pairs, self.rows),
            "col": lax.rem(chip, self.pairs) * 2 + half,
        }

    def beside(self, dr, dc):
        return {"scene": self.scene, "row": self.row + dr, "col": self.col + dc}

    def row_across(self, step):
        span = 2**step
        return self.row + span - 2 * span * lax.rem(self.row // span, 2)

    def plane_before(self, u):
        return lax.rem(self.plane + 2 * self.m - 1 - u, self.m)


def loop(low, high, body, unroll=1):
    def wrapped(j, carry):
        body(j)
        return carry

    lax.fori_loop(low, high, wrapped, 0, unroll=unroll)


def wait_all(ref, sem):
    pltpu.make_async_copy(ref, ref, sem).wait()


def inside(place, dr, dc):
    row, col = place.row + dr, place.col + dc
    fits = jnp.logical_and(row >= 0, row < place.rows)
    return jnp.logical_and(fits, jnp.logical_and(col >= 0, col < place.cols))


def greeted(place, dr, dc):
    if dc:
        return inside(place, dr, dc)
    first = place.row_across(0) if place.doublings else place.row
    return jnp.logical_and(inside(place, dr, dc), first != place.row + dr)


def greet(place):
    barrier = pltpu.get_barrier_semaphore()

    def signal(device):
        pl.semaphore_signal(barrier, inc=1, device_id=device, device_id_type=MESH)

    signal(place.device(place.me, 1 - place.half))
    for dr in (-1, 1):
        for dc in (-1, 0, 1):

            @pl.when(greeted(place, dr, dc))
            def _():
                signal(place.beside(dr, dc))

    def plane_peer(u):
        chip = place.chip(place.plane_after(u), place.row)
        signal(place.device(chip, place.half))
        signal(place.device(chip, 1 - place.half))

    loop(0, place.m - 1, plane_peer)
    for step in range(place.doublings):
        signal(place.device(place.chip(place.plane, place.row_across(step)), place.half))
    expected = jnp.int32(2 * place.m - 1 + place.doublings)
    for dr in (-1, 1):
        for dc in (-1, 0, 1):
            expected = expected + greeted(place, dr, dc).astype(jnp.int32)
    return barrier, expected


AROUND = tuple((dr, dc) for dr in (-1, 0, 1) for dc in (-1, 0, 1) if dr or dc)


def edge_of(dr, dc):
    if dr:
        return 1 if dr < 0 else 0
    return 3 if dc < 0 else 2


def halo_copies(place, edges, halo, halo_send, halo_recv):
    copies = []
    for slot, (dr, dc) in enumerate(AROUND):
        src, dst = edges.at[edge_of(dr, dc)], halo.at[slot]
        if dr and dc:
            width = edges.shape[2]
            part = pl.ds(width - 16, 16) if dc < 0 else pl.ds(0, 16)
            src, dst = src.at[:, part], dst.at[:, part]
        copy = pltpu.make_async_remote_copy(
            src_ref=src,
            dst_ref=dst,
            send_sem=halo_send.at[slot],
            recv_sem=halo_recv.at[slot],
            device_id=place.beside(-dr, -dc),
            device_id_type=MESH,
        )
        copies.append((copy, inside(place, -dr, -dc), inside(place, dr, dc)))
    return copies


def fill(place, which, cells, halo, cat, cols):
    height, width, channels = cells.shape

    def arrived(dr, dc):
        block = halo[AROUND.index((dr, dc)), which].astype(jnp.float32)
        return jnp.where(inside(place, dr, dc), block, 0.0)

    position = lax.broadcasted_iota(jnp.int32, (width, channels), 0)

    def put(r, line, left, right):
        before = jnp.where(position == 0, left, pltpu.roll(line, 1, 0))
        behind = jnp.where(position == width - 1, right, pltpu.roll(line, width - 1, 0))
        cat[r, :, 0:channels] = before.astype(cat.dtype)
        cat[r, :, channels : 2 * channels] = line.astype(cat.dtype)
        cat[r, :, 2 * channels : 3 * channels] = behind.astype(cat.dtype)

    cols[0] = arrived(0, -1)
    cols[1] = arrived(0, 1)
    for dr, r in ((-1, 0), (1, height + 1)):
        put(r, arrived(dr, 0), arrived(dr, -1)[width - 1 : width], arrived(dr, 1)[0:1])

    def inner(r):
        put(r + 1, cells[r].astype(jnp.float32), cols[0, pl.ds(r, 1), :], cols[1, pl.ds(r, 1), :])

    loop(0, height, inner, unroll=4)


def row_pairs(cat, layer, start, pairs):
    width, channels = cat.shape[2:]
    return jnp.concatenate(
        [jnp.concatenate([cat[layer, start + 2 * p + a] for p in range(pairs)], axis=0) for a in range(4)], axis=1
    )


def kernel(sizes, block_rows, data, params, scenes_hbm, cotangent_hbm, out,
           scenes, cotangent, edges, halo, cat, cols, flat, weights, outs, across, local,
           own, square, squares,
           theirs, sums, landed, kept, run, line_in, line_out,
           whole_own, whole_other, params_own, params_other,
           theirs_b, sums_b, landed_b, kept_b, passed_b, reached_b,
           load_sem, halo_send, halo_recv,
           swap_send, swap_recv, plane_send, plane_recv, line_send, line_recv,
           sq_send, sq_recv, gather_send, gather_recv, relay_send, relay_recv,
           pass_send, pass_recv, params_send, params_recv, carry_send, carry_recv,
           swap_send_b, swap_recv_b, plane_send_b, plane_recv_b, row_send_b, row_recv_b):
    place = Place(sizes)
    n, m, lines, me, half = place.n, place.m, place.rows, place.me, place.half
    height, width, channels = scenes.shape
    rows = params.shape[0]
    taps = 9
    full, half_type = jnp.float32, jnp.bfloat16
    partner = place.device(me, 1 - half)

    def remote(src, dst, send_sem, recv_sem, device):
        return pltpu.make_async_remote_copy(
            src_ref=src, dst_ref=dst, send_sem=send_sem, recv_sem=recv_sem,
            device_id=device, device_id_type=MESH,
        )

    def plane_device(u, to_half):
        return place.device(place.chip(place.plane_after(u), place.row), to_half)

    loads = [
        pltpu.make_async_copy(scenes_hbm, scenes, load_sem.at[0]),
        pltpu.make_async_copy(cotangent_hbm, cotangent, load_sem.at[1]),
    ]

    load_own = pltpu.make_async_copy(data.at[:, :, :, half], own, load_sem.at[3])
    barrier, expected = greet(place)
    load_params = pltpu.make_async_copy(params, params_own.at[place.row, place.plane], load_sem.at[2])
    load_params.start()
    load_own.start()
    for load in loads:
        load.start()
    for layer in range(2):
        weights[layer, 9 * channels : 12 * channels, 0:channels] = jnp.zeros((3 * channels, channels), half_type)
        weights[layer, 0 : 3 * channels, channels : 2 * channels] = jnp.zeros((3 * channels, channels), half_type)
    pl.semaphore_wait(barrier, expected)

    def swap(t):
        return remote(data.at[:, t, :, 1 - half], theirs.at[t], swap_send, swap_recv.at[t], partner)

    loop(0, lines, lambda t: swap(t).start())

    def row_device(step):
        return place.device(place.chip(place.plane, place.row_across(step)), half)

    def passing(step, row):
        block = params_own.at[row, place.plane]
        return remote(block, block, pass_send, pass_recv.at[step], row_device(step))

    load_params.wait()
    for step in range(place.doublings):
        passing(step, place.row).start()

    def others(step):
        span = 2**step
        first = place.row // span * span
        return [first + lax.rem(place.row - first + k, span) for k in range(1, span)]

    def pass_on_params(step):
        for row in others(step):
            passing(step, row).start()

    def params_come(step):
        wait_all(params_own.at[pl.ds(0, 2**step), 0], pass_recv.at[step])

    load_own.wait()

    def both(t, plane):
        scene, pair = plane // place.pairs, lax.rem(plane, place.pairs)
        return own[scene, t, pair] + theirs[t, scene, pair]

    def across_plane(t):
        swap(t).wait_recv()

        def pass_on(u):
            slot = t * (m - 1) + u
            sums[slot] = both(t, place.plane_after(u)).astype(sums.dtype)
            remote(sums.at[slot], landed.at[t, u], plane_send, plane_recv.at[t], plane_device(u, half)).start()

        loop(0, m - 1, pass_on)
        kept[t] = both(t, place.plane)

    loop(0, lines, across_plane)

    for which, (load, cells) in enumerate(zip(loads, (scenes, cotangent))):
        load.wait()
        edges[0, which] = cells[0]
        edges[1, which] = cells[height - 1]
        edges[2, which] = cells[:, 0:16, :].astype(full)[:, 0, :].astype(edges.dtype)
        edges[3, which] = cells[:, width - 16 : width, :].astype(full)[:, 15, :].astype(edges.dtype)
    halos = halo_copies(place, edges, halo, halo_send, halo_recv)
    for copy, out_of, into in halos:
        pl.when(out_of)(copy.start)

    def along(step, t):
        return remote(line_out.at[step, t], line_in.at[step, t], line_send, line_recv.at[step, t], row_device(step))

    side = me // (n // 2)
    near_count = m // 2

    def towards(k, sign):
        near = side * near_count + lax.rem(place.plane + near_count * 2 + sign * (k + 1), near_count)
        far = (1 - side) * near_count + lax.rem(place.plane + near_count * 2 + sign * k, near_count)
        return near, far

    def give(plane, slot, t):
        mine = whole_own.at[t, place.plane]
        device = place.device(place.chip(plane, place.row), half)
        return remote(mine, mine, gather_send, gather_recv.at[t, slot], device)

    def relay(t, plane, far):
        return remote(whole_own.at[t, plane], whole_other.at[t, plane], relay_send, relay_recv.at[far], partner)

    def give_near(t):
        loop(0, near_count - 1, lambda k: give(towards(k, 1)[0], k, t).start())

    def give_far(i):
        t, k = i // near_count, lax.rem(i, near_count)
        give(towards(k, 1)[1], near_count - 1 + k, t).start()

    def give_params(row):
        block = params_own.at[row, place.plane]

        def to(plane, far):
            device = place.device(place.chip(plane, place.row), half)
            remote(block, block, params_send, params_recv.at[far], device).start()

        loop(0, near_count - 1, lambda k: to(towards(k, 1)[0], 0))
        loop(0, near_count, lambda k: to(towards(k, 1)[1], 1))

    def carry(far):
        first = jnp.where(far == 1, 1 - side, side) * near_count
        planes = pl.ds(first, near_count)
        return remote(params_own.at[:, planes], params_other.at[:, planes], carry_send, carry_recv.at[far], partner)

    def share(step, t, total):
        run[t] = total
        if step < place.doublings:
            line_out[step, t] = total.astype(half_type)
            along(step, t).start()
        else:
            whole_own[t, place.plane] = total.astype(half_type)
            give_near(t)
            relay(t, place.plane, 0).start()

    def plane_sum(t):
        wait_all(landed.at[t], plane_recv.at[t])
        share(0, t, lax.fori_loop(0, m - 1, lambda u, sofar: sofar + landed[t, u].astype(full), kept[t]))

    def line_sum(step, t):
        along(step, t).wait_recv()
        share(step + 1, t, run[t] + line_in[step, t].astype(full))

    give_params(place.row)
    if place.doublings:
        params_come(0)
        give_params(place.row_across(0))
    if place.doublings > 1:
        pass_on_params(1)
    loop(0, lines, plane_sum)
    if place.doublings:
        loop(0, lines, functools.partial(line_sum, 0))
    for step in range(1, place.doublings):
        if step > 1:
            pass_on_params(step)
        params_come(step)
        first = place.row_across(step) // 2**step * 2**step
        for k in range(2**step):
            give_params(first + k)
    for copy, out_of, into in halos:
        pl.when(into)(copy.wait_recv)
    fill(place, 0, scenes, halo, cat.at[0], cols)
    for step in range(1, place.doublings):
        loop(0, lines, functools.partial(line_sum, step))
    square[0] = jnp.sum(lax.fori_loop(0, lines, lambda t, sofar: sofar + run[t] * run[t], jnp.zeros((rows, LANES), full)), axis=0, keepdims=True)

    def arrive(t, plane, slot, far):
        there = whole_own.at[t, plane]
        remote(there, there, gather_send, gather_recv.at[t, slot], partner).wait_recv()
        relay(t, plane, far).start()

    def from_near(i):
        t, k = i // (near_count - 1), lax.rem(i, near_count - 1)
        arrive(t, towards(k, -1)[0], k, 0)

    def from_far(i):
        t, k = i // near_count, lax.rem(i, near_count)
        arrive(t, towards(k, -1)[1], near_count - 1 + k, 1)

    def tell(device, slot):
        return remote(square.at[0], squares.at[slot], sq_send, sq_recv, device)

    def tell_chip(u):
        tell(plane_device(u, half), 2 * u + 1).start()
        tell(plane_device(u, 1 - half), 2 * u + 2).start()

    loop(0, m - 1, tell_chip)
    tell(partner, 0).start()
    loop(0, lines * near_count, give_far)
    fill(place, 1, cotangent, halo, cat.at[1], cols)
    wait_all(params_own.at[:, pl.ds(0, near_count - 1)], params_recv.at[0])
    carry(0).start()
    wait_all(params_own.at[:, pl.ds(0, near_count)], params_recv.at[1])
    carry(1).start()
    loop(0, lines * (near_count - 1), from_near)
    wait_all(squares, sq_recv)
    norm2 = jnp.sum(square[0] + jnp.sum(squares[...], axis=0))
    factor = radius / (jnp.sqrt(jnp.full((1, LANES), norm2, full)) + epsilon)

    def spread(layer, i):
        t, plane = i // near_count, layer * near_count + lax.rem(i, near_count)
        c = 2 * place.chip(plane, t)
        flat[pl.ds((c + half) * rows, rows), :] = params_own[t, plane] + factor * whole_own[t, plane].astype(full)
        flat[pl.ds((c + 1 - half) * rows, rows), :] = params_other[t, plane] + factor * whole_other[t, plane].astype(full)

    def put(layer, t, kernel):
        weights[layer, t * channels : (t + 1) * channels, 0:channels] = kernel
        weights[layer, (t + 3) * channels : (t + 4) * channels, channels : 2 * channels] = kernel

    def weigh(layer):
        far = jnp.where(layer == side, 0, 1)
        wait_all(params_other.at[:, pl.ds(0, near_count)], carry_recv.at[far])
        wait_all(whole_other.at[:, pl.ds(0, near_count)], relay_recv.at[far])
        loop(0, lines * near_count, functools.partial(spread, layer), unroll=4)

        @pl.when(layer == 0)
        def _():
            for t in range(taps):
                put(0, t, flat[t * channels : (t + 1) * channels].astype(half_type))

        @pl.when(layer == 1)
        def _():
            for t in range(taps):
                first = (2 * taps - 1 - t) * channels
                put(1, t, flat[first : first + channels].T.astype(half_type))

    blocks, pairs = height // block_rows, block_rows // 2

    def convolve(layer, i):
        start = i * block_rows
        pair = jnp.dot(row_pairs(cat, layer, start, pairs), weights[layer], preferred_element_type=full)
        both_rows = []
        for p in range(pairs):
            part = pair[p * width : (p + 1) * width]
            both_rows.append(jnp.concatenate([part[:, 0:channels], part[:, channels:]], axis=0))
        return start, both_rows

    def convolve_near(i):
        start, both_rows = convolve(side, i)
        for p, cells in enumerate(both_rows):
            outs[pl.ds(start + 2 * p, 2)] = cells.reshape(2, width, channels)

    def convolve_far(i):
        start, both_rows = convolve(1 - side, i)
        for p, cells in enumerate(both_rows):
            near = outs[pl.ds(start + 2 * p, 2)].reshape(2 * width, channels)
            pre = jnp.where(side == 0, near, cells)
            back = jnp.where(side == 0, cells, near)
            squash = jax.nn.sigmoid(pre)
            at = pl.ds(pl.multiple_of((start + 2 * p) * width, 2 * width), 2 * width)
            across[0, :, at] = (back * squash * (1.0 + pre * (1.0 - squash))).T.astype(half_type)
            across[1, :, at] = (pre * squash).T.astype(half_type)

    def take_far():
        loop(0, lines * near_count, from_far)

    pl.when(half == 1)(take_far)
    weigh(side)
    def near_block(i):
        pl.when(jnp.logical_and(i == blocks // 2, half == 0))(take_far)
        convolve_near(i)

    loop(0, blocks, near_block)
    weigh(1 - side)
    loop(0, blocks, convolve_far)

    def field_grad(group):
        for layer in range(2):
            field = jnp.concatenate([
                cat[layer, u // 3 : u // 3 + height, :, u % 3 * channels : (u % 3 + 1) * channels].reshape(height * width, channels)
                for u in group
            ], axis=1)
            grad = jnp.dot(across[layer], field, preferred_element_type=full)
            for i, u in enumerate(group):
                tap = grad[:, i * channels : (i + 1) * channels]
                if layer == 0:
                    flat[u * channels : (u + 1) * channels] = tap.T
                else:
                    t = 2 * taps - 1 - u
                    flat[t * channels : (t + 1) * channels] = tap

    def ready(i, c):
        for h in range(2):
            local[c, h] = flat[pl.ds((2 * c + h) * rows, rows), :]
        remote(local.at[c, 1 - half], theirs_b.at[c], swap_send_b, swap_recv_b.at[i], partner).start()

    def pass_b(c):
        plane = c // (lines * place.pairs) * place.pairs + lax.rem(c, place.pairs)
        row = lax.rem(c // place.pairs, lines)
        total = local[c, half] + theirs_b[c]

        @pl.when(plane == place.plane)
        def _():
            kept_b[row] = total

        @pl.when(plane != place.plane)
        def _():
            u = lax.rem(plane - place.plane - 1 + m, m)
            sums_b[c] = total.astype(half_type)
            remote(sums_b.at[c], landed_b.at[row, u], plane_send_b, plane_recv_b.at[row], plane_device(u, half)).start()

    def completed_by(c):
        touched = range(2 * c * rows // channels, (2 * (c + 1) * rows - 1) // channels + 1)
        return max(i for i, group in enumerate(TAP_GROUPS) if any(t in group for t in touched))

    def each_chunk(chunks, body):
        def mirrored(c):
            body(c)
            body(n - 1 - c)

        starts = [c for c in chunks if c - 1 not in chunks]
        ends = [c + 1 for c in chunks if c + 1 not in chunks]
        for low, high in zip(starts, ends):
            loop(low, high, mirrored)

    completed = [[c for c in range(n // 2) if completed_by(c) == i] for i in range(len(TAP_GROUPS))]

    def pass_group(i):
        wait_all(theirs_b.at[pl.ds(0, 2 * len(completed[i]))], swap_recv_b.at[i])
        each_chunk(completed[i], pass_b)

    for i, group in enumerate(TAP_GROUPS):
        field_grad(group)
        if i:
            pass_group(i - 1)
        each_chunk(completed[i], functools.partial(ready, i))
    pass_group(len(TAP_GROUPS) - 1)

    def along_rows(k):
        row = jnp.where(side == 0, k, lines - 1 - k)
        wait_all(landed_b.at[row], plane_recv_b.at[row])
        total = lax.fori_loop(0, m - 1, lambda u, sofar: sofar + landed_b[row, u].astype(full), kept_b[row])
        kept_b[row] = total

        @pl.when(row != place.row)
        def _():
            t = lax.rem(row - place.row - 1 + lines, lines)
            passed_b[t] = total.astype(half_type)
            device = place.device(place.chip(place.plane, row), half)
            remote(passed_b.at[t], reached_b.at[t], row_send_b, row_recv_b, device).start()

    loop(0, lines, along_rows)
    wait_all(theirs, swap_send)
    wait_all(sums, plane_send)
    wait_all(squares, sq_send)
    wait_all(whole_other, relay_send)
    wait_all(params_own.at[pl.ds(0, lines - 1), 0], pass_send)
    wait_all(params_own.at[:, pl.ds(0, m - 1)], params_send)
    wait_all(params_own, carry_send)
    wait_all(whole_own.at[:, pl.ds(0, m - 1)], gather_send)
    for copy, out_of, into in halos:
        pl.when(out_of)(copy.wait_send)
    if place.doublings:
        wait_all(line_out, line_send)
    wait_all(theirs_b, swap_send_b)
    wait_all(sums_b.at[pl.ds(0, n - lines)], plane_send_b)
    wait_all(reached_b, row_recv_b)
    out[...] = lax.fori_loop(0, lines - 1, lambda t, sofar: sofar + reached_b[t].astype(full), kept_b[place.row])
    wait_all(reached_b, row_send_b)


def on_device(sizes, scenes, cotangent, params, partials):
    scenes, cotangent = scenes[0], cotangent[0]
    height, width, channels = scenes.shape
    n = sizes[0] * sizes[1] * sizes[2] // 2
    rows = params.size // LANES
    dma = pltpu.SemaphoreType.DMA
    half_type, full = jnp.bfloat16, jnp.float32
    anywhere, vmem = pl.BlockSpec(memory_space=pl.ANY), pl.BlockSpec(memory_space=pltpu.VMEM)
    lines, m = sizes[1], n // sizes[1]
    one = (rows, LANES)
    doublings = max((lines - 1).bit_length(), 1)
    scratch = [
        pltpu.VMEM(scenes.shape, half_type),
        pltpu.VMEM(scenes.shape, half_type),
        pltpu.VMEM((4, 2, width, channels), half_type),
        pltpu.VMEM((len(AROUND), 2, width, channels), half_type),
        pltpu.VMEM((2, height + 2, width, 3 * channels), half_type),
        pltpu.VMEM((2, height, channels), full),
        pltpu.VMEM((18 * channels, channels), full),
        pltpu.VMEM((2, 12 * channels, 2 * channels), half_type),
        pltpu.VMEM((height, width, channels), full),
        pltpu.VMEM((2, channels, height * width), half_type),
        pltpu.VMEM((n, 2, *one), full),
        pltpu.VMEM((sizes[0], lines, sizes[2] // 2, *one), full),
        pltpu.VMEM((1, 1, LANES), full),
        pltpu.VMEM((2 * m - 1, 1, LANES), full),
        pltpu.VMEM((lines, sizes[0], sizes[2] // 2, *one), full),
        pltpu.VMEM((n - lines, *one), half_type),
        pltpu.VMEM((lines, m - 1, *one), half_type),
        pltpu.VMEM((lines, *one), full),
        pltpu.VMEM((lines, *one), full),
        pltpu.VMEM((doublings, lines, *one), half_type),
        pltpu.VMEM((doublings, lines, *one), half_type),
        pltpu.VMEM((lines, m, *one), half_type),
        pltpu.VMEM((lines, m, *one), half_type),
        pltpu.VMEM((lines, m, *one), full),
        pltpu.VMEM((lines, m, *one), full),
        pltpu.VMEM((n, *one), full),
        pltpu.VMEM((n, *one), half_type),
        pltpu.VMEM((lines, m - 1, *one), half_type),
        pltpu.VMEM((lines, *one), full),
        pltpu.VMEM((lines - 1, *one), half_type),
        pltpu.VMEM((lines - 1, *one), half_type),
        dma((4,)), dma((len(AROUND),)), dma((len(AROUND),)),
        dma, dma((lines,)), dma, dma((lines,)), dma, dma((doublings, lines)),
        dma, dma, dma, dma((lines, m - 1)), dma, dma((2,)),
        dma, dma((doublings,)), dma, dma((2,)), dma, dma((2,)),
        dma, dma((len(TAP_GROUPS),)), dma, dma((lines,)), dma, dma,
    ]
    grads = pl.pallas_call(
        functools.partial(kernel, sizes, 32),
        out_shape=pltpu.VMEM((rows, LANES), full),
        in_specs=[anywhere, anywhere, anywhere, anywhere],
        out_specs=vmem,
        scratch_shapes=scratch,
        compiler_params=pltpu.CompilerParams(
            collective_id=0, has_side_effects=True, vmem_limit_bytes=56 * 2**20
        ),
        name="sam_grad",
    )(partials[0].reshape(sizes[0], lines, sizes[2] // 2, 2, rows, LANES), params.reshape(rows, LANES), scenes, cotangent)
    return grads.reshape(-1)


def solution(mesh):
    sizes = tuple(mesh.shape[axis] for axis in AXES)
    return jax.shard_map(
        functools.partial(on_device, sizes),
        mesh=mesh,
        in_specs=(
            P("scene", "row", "col", None),
            P("scene", "row", "col", None),
            P(AXES),
            P(AXES, None),
        ),
        out_specs=P(AXES),
        check_vma=False,
    )
```

```python
import functools

import jax
import jax.numpy as jnp
from jax import lax
from jax.experimental import pallas as pl
from jax.experimental.pallas import tpu as pltpu
from jax.sharding import PartitionSpec as P

radius = 2.0
epsilon = 1e-06
AXES = ("scene", "row", "col")
MESH = pl.DeviceIdType.MESH
LANES = 128
TAP_GROUPS = ((0, 1, 4, 5), (2, 3, 6, 7), (8,))


class Place:
    def __init__(self, sizes):
        self.scenes, self.rows, self.cols = sizes
        self.pairs = self.cols // 2
        self.n = self.scenes * self.rows * self.pairs
        self.col = col = lax.axis_index("col")
        self.scene = lax.axis_index("scene")
        self.half = lax.rem(col, 2)
        self.m = self.scenes * self.pairs
        self.doublings = (self.rows - 1).bit_length()
        self.row = lax.axis_index("row")
        self.plane = lax.axis_index("scene") * self.pairs + col // 2
        self.me = self.chip(self.plane, self.row)

    def chip(self, plane, row):
        return (plane // self.pairs * self.rows + row) * self.pairs + lax.rem(plane, self.pairs)

    def plane_after(self, u):
        return lax.rem(self.plane + 1 + u, self.m)

    def row_after(self, t):
        return lax.rem(self.row + 1 + t, self.rows)

    def order(self, j):
        return self.chip(self.plane_after(lax.rem(j, self.m)), self.row_after(j // self.m))

    def device(self, chip, half):
        return {
            "scene": chip // (self.rows * self.pairs),
            "row": lax.rem(chip // self.pairs, self.rows),
            "col": lax.rem(chip, self.pairs) * 2 + half,
        }

    def beside(self, dr, dc):
        return {"scene": self.scene, "row": self.row + dr, "col": self.col + dc}

    def row_across(self, step):
        span = 2**step
        return self.row + span - 2 * span * lax.rem(self.row // span, 2)

    def plane_before(self, u):
        return lax.rem(self.plane + 2 * self.m - 1 - u, self.m)


def loop(low, high, body, unroll=1):
    def wrapped(j, carry):
        body(j)
        return carry

    lax.fori_loop(low, high, wrapped, 0, unroll=unroll)


def wait_all(ref, sem):
    pltpu.make_async_copy(ref, ref, sem).wait()


def inside(place, dr, dc):
    row, col = place.row + dr, place.col + dc
    fits = jnp.logical_and(row >= 0, row < place.rows)
    return jnp.logical_and(fits, jnp.logical_and(col >= 0, col < place.cols))


def greeted(place, dr, dc):
    if dc:
        return inside(place, dr, dc)
    first = place.row_across(0) if place.doublings else place.row
    return jnp.logical_and(inside(place, dr, dc), first != place.row + dr)


def greet(place):
    barrier = pltpu.get_barrier_semaphore()

    def signal(device):
        pl.semaphore_signal(barrier, inc=1, device_id=device, device_id_type=MESH)

    signal(place.device(place.me, 1 - place.half))
    for dr in (-1, 1):
        for dc in (-1, 0, 1):

            @pl.when(greeted(place, dr, dc))
            def _():
                signal(place.beside(dr, dc))

    def plane_peer(u):
        chip = place.chip(place.plane_after(u), place.row)
        signal(place.device(chip, place.half))
        signal(place.device(chip, 1 - place.half))

    loop(0, place.m - 1, plane_peer)
    for step in range(place.doublings):
        signal(place.device(place.chip(place.plane, place.row_across(step)), place.half))
    expected = jnp.int32(2 * place.m - 1 + place.doublings)
    for dr in (-1, 1):
        for dc in (-1, 0, 1):
            expected = expected + greeted(place, dr, dc).astype(jnp.int32)
    return barrier, expected


AROUND = tuple((dr, dc) for dr in (-1, 0, 1) for dc in (-1, 0, 1) if dr or dc)


def edge_of(dr, dc):
    if dr:
        return 1 if dr < 0 else 0
    return 3 if dc < 0 else 2


def halo_copies(place, edges, halo, halo_send, halo_recv):
    copies = []
    for slot, (dr, dc) in enumerate(AROUND):
        src, dst = edges.at[edge_of(dr, dc)], halo.at[slot]
        if dr and dc:
            width = edges.shape[2]
            part = pl.ds(width - 16, 16) if dc < 0 else pl.ds(0, 16)
            src, dst = src.at[:, part], dst.at[:, part]
        copy = pltpu.make_async_remote_copy(
            src_ref=src,
            dst_ref=dst,
            send_sem=halo_send.at[slot],
            recv_sem=halo_recv.at[slot],
            device_id=place.beside(-dr, -dc),
            device_id_type=MESH,
        )
        copies.append((copy, inside(place, -dr, -dc), inside(place, dr, dc)))
    return copies


def fill(place, which, cells, halo, cat, cols):
    height, width, channels = cells.shape

    def arrived(dr, dc):
        block = halo[AROUND.index((dr, dc)), which].astype(jnp.float32)
        return jnp.where(inside(place, dr, dc), block, 0.0)

    position = lax.broadcasted_iota(jnp.int32, (width, channels), 0)

    def put(r, line, left, right):
        before = jnp.where(position == 0, left, pltpu.roll(line, 1, 0))
        behind = jnp.where(position == width - 1, right, pltpu.roll(line, width - 1, 0))
        cat[r, :, 0:channels] = before.astype(cat.dtype)
        cat[r, :, channels : 2 * channels] = line.astype(cat.dtype)
        cat[r, :, 2 * channels : 3 * channels] = behind.astype(cat.dtype)

    cols[0] = arrived(0, -1)
    cols[1] = arrived(0, 1)
    for dr, r in ((-1, 0), (1, height + 1)):
        put(r, arrived(dr, 0), arrived(dr, -1)[width - 1 : width], arrived(dr, 1)[0:1])

    def inner(r):
        put(r + 1, cells[r].astype(jnp.float32), cols[0, pl.ds(r, 1), :], cols[1, pl.ds(r, 1), :])

    loop(0, height, inner, unroll=4)


def row_pairs(cat, layer, start, pairs):
    width, channels = cat.shape[2:]
    return jnp.concatenate(
        [jnp.concatenate([cat[layer, start + 2 * p + a] for p in range(pairs)], axis=0) for a in range(4)], axis=1
    )


def kernel(sizes, block_rows, data, params, scenes_hbm, cotangent_hbm, out,
           scenes, cotangent, edges, halo, cat, cols, flat, weights, outs, across, local,
           own, square, squares,
           theirs, sums, landed, kept, run, line_in, line_out,
           whole_own, whole_other, params_own, params_other,
           theirs_b, sums_b, landed_b, kept_b, passed_b, reached_b,
           load_sem, halo_send, halo_recv,
           swap_send, swap_recv, plane_send, plane_recv, line_send, line_recv,
           sq_send, sq_recv, gather_send, gather_recv, relay_send, relay_recv,
           pass_send, pass_recv, params_send, params_recv, carry_send, carry_recv,
           swap_send_b, swap_recv_b, plane_send_b, plane_recv_b, row_send_b, row_recv_b):
    place = Place(sizes)
    n, m, lines, me, half = place.n, place.m, place.rows, place.me, place.half
    height, width, channels = scenes.shape
    rows = params.shape[0]
    taps = 9
    full, half_type = jnp.float32, jnp.bfloat16
    partner = place.device(me, 1 - half)

    def remote(src, dst, send_sem, recv_sem, device):
        return pltpu.make_async_remote_copy(
            src_ref=src, dst_ref=dst, send_sem=send_sem, recv_sem=recv_sem,
            device_id=device, device_id_type=MESH,
        )

    def plane_device(u, to_half):
        return place.device(place.chip(place.plane_after(u), place.row), to_half)

    loads = [
        pltpu.make_async_copy(scenes_hbm, scenes, load_sem.at[0]),
        pltpu.make_async_copy(cotangent_hbm, cotangent, load_sem.at[1]),
    ]

    load_own = pltpu.make_async_copy(data.at[:, :, :, half], own, load_sem.at[3])
    barrier, expected = greet(place)
    load_params = pltpu.make_async_copy(params, params_own.at[place.row, place.plane], load_sem.at[2])
    load_params.start()
    load_own.start()
    for load in loads:
        load.start()
    for layer in range(2):
        weights[layer, 9 * channels : 12 * channels, 0:channels] = jnp.zeros((3 * channels, channels), half_type)
        weights[layer, 0 : 3 * channels, channels : 2 * channels] = jnp.zeros((3 * channels, channels), half_type)
    pl.semaphore_wait(barrier, expected)

    def swap(t):
        return remote(data.at[:, t, :, 1 - half], theirs.at[t], swap_send, swap_recv.at[t], partner)

    loop(0, lines, lambda t: swap(t).start())

    def row_device(step):
        return place.device(place.chip(place.plane, place.row_across(step)), half)

    def passing(step, row):
        block = params_own.at[row, place.plane]
        return remote(block, block, pass_send, pass_recv.at[step], row_device(step))

    load_params.wait()
    for step in range(place.doublings):
        passing(step, place.row).start()

    def others(step):
        span = 2**step
        first = place.row // span * span
        return [first + lax.rem(place.row - first + k, span) for k in range(1, span)]

    def pass_on_params(step):
        for row in others(step):
            passing(step, row).start()

    def params_come(step):
        wait_all(params_own.at[pl.ds(0, 2**step), 0], pass_recv.at[step])

    load_own.wait()

    def both(t, plane):
        scene, pair = plane // place.pairs, lax.rem(plane, place.pairs)
        return own[scene, t, pair] + theirs[t, scene, pair]

    def across_plane(t):
        swap(t).wait_recv()

        def pass_on(u):
            slot = t * (m - 1) + u
            sums[slot] = both(t, place.plane_after(u)).astype(sums.dtype)
            remote(sums.at[slot], landed.at[t, u], plane_send, plane_recv.at[t], plane_device(u, half)).start()

        loop(0, m - 1, pass_on)
        kept[t] = both(t, place.plane)

    loop(0, lines, across_plane)

    for which, (load, cells) in enumerate(zip(loads, (scenes, cotangent))):
        load.wait()
        edges[0, which] = cells[0]
        edges[1, which] = cells[height - 1]
        edges[2, which] = cells[:, 0:16, :].astype(full)[:, 0, :].astype(edges.dtype)
        edges[3, which] = cells[:, width - 16 : width, :].astype(full)[:, 15, :].astype(edges.dtype)
    halos = halo_copies(place, edges, halo, halo_send, halo_recv)
    for copy, out_of, into in halos:
        pl.when(out_of)(copy.start)

    def along(step, t):
        return remote(line_out.at[step, t], line_in.at[step, t], line_send, line_recv.at[step, t], row_device(step))

    side = me // (n // 2)
    near_count = m // 2

    def towards(k, sign):
        near = side * near_count + lax.rem(place.plane + near_count * 2 + sign * (k + 1), near_count)
        far = (1 - side) * near_count + lax.rem(place.plane + near_count * 2 + sign * k, near_count)
        return near, far

    def give(plane, slot, t):
        mine = whole_own.at[t, place.plane]
        device = place.device(place.chip(plane, place.row), half)
        return remote(mine, mine, gather_send, gather_recv.at[t, slot], device)

    def relay(t, plane, far):
        return remote(whole_own.at[t, plane], whole_other.at[t, plane], relay_send, relay_recv.at[far], partner)

    def give_near(t):
        loop(0, near_count - 1, lambda k: give(towards(k, 1)[0], k, t).start())

    def give_far(i):
        t, k = i // near_count, lax.rem(i, near_count)
        give(towards(k, 1)[1], near_count - 1 + k, t).start()

    def give_params(row):
        block = params_own.at[row, place.plane]

        def to(plane, far):
            device = place.device(place.chip(plane, place.row), half)
            remote(block, block, params_send, params_recv.at[far], device).start()

        loop(0, near_count - 1, lambda k: to(towards(k, 1)[0], 0))
        loop(0, near_count, lambda k: to(towards(k, 1)[1], 1))

    def carry(far):
        first = jnp.where(far == 1, 1 - side, side) * near_count
        planes = pl.ds(first, near_count)
        return remote(params_own.at[:, planes], params_other.at[:, planes], carry_send, carry_recv.at[far], partner)

    def share(step, t, total):
        run[t] = total
        if step < place.doublings:
            line_out[step, t] = total.astype(half_type)
            along(step, t).start()
        else:
            whole_own[t, place.plane] = total.astype(half_type)
            give_near(t)
            relay(t, place.plane, 0).start()

    def plane_sum(t):
        wait_all(landed.at[t], plane_recv.at[t])
        share(0, t, lax.fori_loop(0, m - 1, lambda u, sofar: sofar + landed[t, u].astype(full), kept[t]))

    def line_sum(step, t):
        along(step, t).wait_recv()
        share(step + 1, t, run[t] + line_in[step, t].astype(full))

    give_params(place.row)
    if place.doublings:
        params_come(0)
        give_params(place.row_across(0))
    if place.doublings > 1:
        pass_on_params(1)
    def more_params(step):
        if step > 1:
            pass_on_params(step)
        params_come(step)
        first = place.row_across(step) // 2**step * 2**step
        for k in range(2**step):
            give_params(first + k)

    loop(0, lines, plane_sum)
    if place.doublings > 1:
        more_params(1)
    if place.doublings:
        loop(0, lines, functools.partial(line_sum, 0))
    for step in range(2, place.doublings):
        more_params(step)
    for copy, out_of, into in halos:
        pl.when(into)(copy.wait_recv)
    fill(place, 0, scenes, halo, cat.at[0], cols)
    for step in range(1, place.doublings):
        loop(0, lines, functools.partial(line_sum, step))
    square[0] = jnp.sum(lax.fori_loop(0, lines, lambda t, sofar: sofar + run[t] * run[t], jnp.zeros((rows, LANES), full)), axis=0, keepdims=True)

    def arrive(t, plane, slot, far):
        there = whole_own.at[t, plane]
        remote(there, there, gather_send, gather_recv.at[t, slot], partner).wait_recv()
        relay(t, plane, far).start()

    def from_near(i):
        t, k = i // (near_count - 1), lax.rem(i, near_count - 1)
        arrive(t, towards(k, -1)[0], k, 0)

    def from_far(i):
        t, k = i // near_count, lax.rem(i, near_count)
        arrive(t, towards(k, -1)[1], near_count - 1 + k, 1)

    def tell(device, slot):
        return remote(square.at[0], squares.at[slot], sq_send, sq_recv, device)

    def tell_chip(u):
        tell(plane_device(u, half), 2 * u + 1).start()
        tell(plane_device(u, 1 - half), 2 * u + 2).start()

    loop(0, m - 1, tell_chip)
    tell(partner, 0).start()
    loop(0, lines * near_count, give_far)
    fill(place, 1, cotangent, halo, cat.at[1], cols)
    wait_all(params_own.at[:, pl.ds(0, near_count - 1)], params_recv.at[0])
    carry(0).start()
    wait_all(params_own.at[:, pl.ds(0, near_count)], params_recv.at[1])
    carry(1).start()
    loop(0, lines * (near_count - 1), from_near)
    wait_all(squares, sq_recv)
    norm2 = jnp.sum(square[0] + jnp.sum(squares[...], axis=0))
    factor = radius / (jnp.sqrt(jnp.full((1, LANES), norm2, full)) + epsilon)

    def spread(layer, i):
        t, plane = i // near_count, layer * near_count + lax.rem(i, near_count)
        c = 2 * place.chip(plane, t)
        flat[pl.ds((c + half) * rows, rows), :] = params_own[t, plane] + factor * whole_own[t, plane].astype(full)
        flat[pl.ds((c + 1 - half) * rows, rows), :] = params_other[t, plane] + factor * whole_other[t, plane].astype(full)

    def put(layer, t, kernel):
        weights[layer, t * channels : (t + 1) * channels, 0:channels] = kernel
        weights[layer, (t + 3) * channels : (t + 4) * channels, channels : 2 * channels] = kernel

    def weigh(layer):
        far = jnp.where(layer == side, 0, 1)
        wait_all(params_other.at[:, pl.ds(0, near_count)], carry_recv.at[far])
        wait_all(whole_other.at[:, pl.ds(0, near_count)], relay_recv.at[far])
        loop(0, lines * near_count, functools.partial(spread, layer), unroll=4)

        @pl.when(layer == 0)
        def _():
            for t in range(taps):
                put(0, t, flat[t * channels : (t + 1) * channels].astype(half_type))

        @pl.when(layer == 1)
        def _():
            for t in range(taps):
                first = (2 * taps - 1 - t) * channels
                put(1, t, flat[first : first + channels].T.astype(half_type))

    blocks, pairs = height // block_rows, block_rows // 2

    def convolve(layer, i):
        start = i * block_rows
        pair = jnp.dot(row_pairs(cat, layer, start, pairs), weights[layer], preferred_element_type=full)
        both_rows = []
        for p in range(pairs):
            part = pair[p * width : (p + 1) * width]
            both_rows.append(jnp.concatenate([part[:, 0:channels], part[:, channels:]], axis=0))
        return start, both_rows

    def convolve_near(i):
        start, both_rows = convolve(side, i)
        for p, cells in enumerate(both_rows):
            outs[pl.ds(start + 2 * p, 2)] = cells.reshape(2, width, channels)

    def convolve_far(i):
        start, both_rows = convolve(1 - side, i)
        for p, cells in enumerate(both_rows):
            near = outs[pl.ds(start + 2 * p, 2)].reshape(2 * width, channels)
            pre = jnp.where(side == 0, near, cells)
            back = jnp.where(side == 0, cells, near)
            squash = jax.nn.sigmoid(pre)
            at = pl.ds(pl.multiple_of((start + 2 * p) * width, 2 * width), 2 * width)
            across[0, :, at] = (back * squash * (1.0 + pre * (1.0 - squash))).T.astype(half_type)
            across[1, :, at] = (pre * squash).T.astype(half_type)

    def take_far():
        loop(0, lines * near_count, from_far)

    pl.when(half == 1)(take_far)
    weigh(side)
    def near_block(i):
        pl.when(jnp.logical_and(i == blocks // 2, half == 0))(take_far)
        convolve_near(i)

    loop(0, blocks, near_block)
    weigh(1 - side)
    loop(0, blocks, convolve_far)

    def field_grad(group, layers=(0, 1)):
        for layer in layers:
            field = jnp.concatenate([
                cat[layer, u // 3 : u // 3 + height, :, u % 3 * channels : (u % 3 + 1) * channels].reshape(height * width, channels)
                for u in group
            ], axis=1)
            grad = jnp.dot(across[layer], field, preferred_element_type=full)
            for i, u in enumerate(group):
                tap = grad[:, i * channels : (i + 1) * channels]
                if layer == 0:
                    flat[u * channels : (u + 1) * channels] = tap.T
                else:
                    t = 2 * taps - 1 - u
                    flat[t * channels : (t + 1) * channels] = tap

    def ready(i, c):
        for h in range(2):
            local[c, h] = flat[pl.ds((2 * c + h) * rows, rows), :]
        remote(local.at[c, 1 - half], theirs_b.at[c], swap_send_b, swap_recv_b.at[i], partner).start()

    def pass_b(c):
        plane = c // (lines * place.pairs) * place.pairs + lax.rem(c, place.pairs)
        row = lax.rem(c // place.pairs, lines)
        total = local[c, half] + theirs_b[c]

        @pl.when(plane == place.plane)
        def _():
            kept_b[row] = total

        @pl.when(plane != place.plane)
        def _():
            u = lax.rem(plane - place.plane - 1 + m, m)
            sums_b[c] = total.astype(half_type)
            remote(sums_b.at[c], landed_b.at[row, u], plane_send_b, plane_recv_b.at[row], plane_device(u, half)).start()

    def completed_by(c):
        touched = range(2 * c * rows // channels, (2 * (c + 1) * rows - 1) // channels + 1)
        return max(i for i, group in enumerate(TAP_GROUPS) if any(t in group for t in touched))

    def each_chunk(chunks, body):
        def mirrored(c):
            body(c)
            body(n - 1 - c)

        starts = [c for c in chunks if c - 1 not in chunks]
        ends = [c + 1 for c in chunks if c + 1 not in chunks]
        for low, high in zip(starts, ends):
            loop(low, high, mirrored)

    completed = [[c for c in range(n // 2) if completed_by(c) == i] for i in range(len(TAP_GROUPS))]

    def pass_group(i):
        wait_all(theirs_b.at[pl.ds(0, 2 * len(completed[i]))], swap_recv_b.at[i])
        each_chunk(completed[i], pass_b)

    for i, group in enumerate(TAP_GROUPS):
        field_grad(group)
        each_chunk(completed[i], functools.partial(ready, i))
        if i:
            pass_group(i - 1)
    pass_group(len(TAP_GROUPS) - 1)

    def along_rows(k):
        row = jnp.where(side == 0, k, lines - 1 - k)
        wait_all(landed_b.at[row], plane_recv_b.at[row])
        total = lax.fori_loop(0, m - 1, lambda u, sofar: sofar + landed_b[row, u].astype(full), kept_b[row])
        kept_b[row] = total

        @pl.when(row != place.row)
        def _():
            t = lax.rem(row - place.row - 1 + lines, lines)
            passed_b[t] = total.astype(half_type)
            device = place.device(place.chip(place.plane, row), half)
            remote(passed_b.at[t], reached_b.at[t], row_send_b, row_recv_b, device).start()

    loop(0, lines, along_rows)
    wait_all(theirs, swap_send)
    wait_all(sums, plane_send)
    wait_all(squares, sq_send)
    wait_all(whole_other, relay_send)
    wait_all(params_own.at[pl.ds(0, lines - 1), 0], pass_send)
    wait_all(params_own.at[:, pl.ds(0, m - 1)], params_send)
    wait_all(params_own, carry_send)
    wait_all(whole_own.at[:, pl.ds(0, m - 1)], gather_send)
    for copy, out_of, into in halos:
        pl.when(out_of)(copy.wait_send)
    if place.doublings:
        wait_all(line_out, line_send)
    wait_all(theirs_b, swap_send_b)
    wait_all(sums_b.at[pl.ds(0, n - lines)], plane_send_b)
    wait_all(reached_b, row_recv_b)
    out[...] = lax.fori_loop(0, lines - 1, lambda t, sofar: sofar + reached_b[t].astype(full), kept_b[place.row])
    wait_all(reached_b, row_send_b)


def on_device(sizes, scenes, cotangent, params, partials):
    scenes, cotangent = scenes[0], cotangent[0]
    height, width, channels = scenes.shape
    n = sizes[0] * sizes[1] * sizes[2] // 2
    rows = params.size // LANES
    dma = pltpu.SemaphoreType.DMA
    half_type, full = jnp.bfloat16, jnp.float32
    anywhere, vmem = pl.BlockSpec(memory_space=pl.ANY), pl.BlockSpec(memory_space=pltpu.VMEM)
    lines, m = sizes[1], n // sizes[1]
    one = (rows, LANES)
    doublings = max((lines - 1).bit_length(), 1)
    scratch = [
        pltpu.VMEM(scenes.shape, half_type),
        pltpu.VMEM(scenes.shape, half_type),
        pltpu.VMEM((4, 2, width, channels), half_type),
        pltpu.VMEM((len(AROUND), 2, width, channels), half_type),
        pltpu.VMEM((2, height + 2, width, 3 * channels), half_type),
        pltpu.VMEM((2, height, channels), full),
        pltpu.VMEM((18 * channels, channels), full),
        pltpu.VMEM((2, 12 * channels, 2 * channels), half_type),
        pltpu.VMEM((height, width, channels), full),
        pltpu.VMEM((2, channels, height * width), half_type),
        pltpu.VMEM((n, 2, *one), full),
        pltpu.VMEM((sizes[0], lines, sizes[2] // 2, *one), full),
        pltpu.VMEM((1, 1, LANES), full),
        pltpu.VMEM((2 * m - 1, 1, LANES), full),
        pltpu.VMEM((lines, sizes[0], sizes[2] // 2, *one), full),
        pltpu.VMEM((n - lines, *one), half_type),
        pltpu.VMEM((lines, m - 1, *one), half_type),
        pltpu.VMEM((lines, *one), full),
        pltpu.VMEM((lines, *one), full),
        pltpu.VMEM((doublings, lines, *one), half_type),
        pltpu.VMEM((doublings, lines, *one), half_type),
        pltpu.VMEM((lines, m, *one), half_type),
        pltpu.VMEM((lines, m, *one), half_type),
        pltpu.VMEM((lines, m, *one), full),
        pltpu.VMEM((lines, m, *one), full),
        pltpu.VMEM((n, *one), full),
        pltpu.VMEM((n, *one), half_type),
        pltpu.VMEM((lines, m - 1, *one), half_type),
        pltpu.VMEM((lines, *one), full),
        pltpu.VMEM((lines - 1, *one), half_type),
        pltpu.VMEM((lines - 1, *one), half_type),
        dma((4,)), dma((len(AROUND),)), dma((len(AROUND),)),
        dma, dma((lines,)), dma, dma((lines,)), dma, dma((doublings, lines)),
        dma, dma, dma, dma((lines, m - 1)), dma, dma((2,)),
        dma, dma((doublings,)), dma, dma((2,)), dma, dma((2,)),
        dma, dma((len(TAP_GROUPS),)), dma, dma((lines,)), dma, dma,
    ]
    grads = pl.pallas_call(
        functools.partial(kernel, sizes, 32),
        out_shape=pltpu.VMEM((rows, LANES), full),
        in_specs=[anywhere, anywhere, anywhere, anywhere],
        out_specs=vmem,
        scratch_shapes=scratch,
        compiler_params=pltpu.CompilerParams(
            collective_id=0, has_side_effects=True, vmem_limit_bytes=56 * 2**20
        ),
        name="sam_grad",
    )(partials[0].reshape(sizes[0], lines, sizes[2] // 2, 2, rows, LANES), params.reshape(rows, LANES), scenes, cotangent)
    return grads.reshape(-1)


def solution(mesh):
    sizes = tuple(mesh.shape[axis] for axis in AXES)
    return jax.shard_map(
        functools.partial(on_device, sizes),
        mesh=mesh,
        in_specs=(
            P("scene", "row", "col", None),
            P("scene", "row", "col", None),
            P(AXES),
            P(AXES, None),
        ),
        out_specs=P(AXES),
        check_vma=False,
    )
```

```python
import functools

import jax
import jax.numpy as jnp
from jax import lax
from jax.experimental import pallas as pl
from jax.experimental.pallas import tpu as pltpu
from jax.sharding import PartitionSpec as P

radius = 2.0
epsilon = 1e-06
AXES = ("scene", "row", "col")
MESH = pl.DeviceIdType.MESH
LANES = 128
TAP_GROUPS = ((0, 1, 4, 5), (2, 3, 6, 7), (8,))


class Place:
    def __init__(self, sizes):
        self.scenes, self.rows, self.cols = sizes
        self.pairs = self.cols // 2
        self.n = self.scenes * self.rows * self.pairs
        self.col = col = lax.axis_index("col")
        self.scene = lax.axis_index("scene")
        self.half = lax.rem(col, 2)
        self.m = self.scenes * self.pairs
        self.doublings = (self.rows - 1).bit_length()
        self.row = lax.axis_index("row")
        self.plane = lax.axis_index("scene") * self.pairs + col // 2
        self.me = self.chip(self.plane, self.row)

    def chip(self, plane, row):
        return (plane // self.pairs * self.rows + row) * self.pairs + lax.rem(plane, self.pairs)

    def plane_after(self, u):
        return lax.rem(self.plane + 1 + u, self.m)

    def row_after(self, t):
        return lax.rem(self.row + 1 + t, self.rows)

    def order(self, j):
        return self.chip(self.plane_after(lax.rem(j, self.m)), self.row_after(j // self.m))

    def device(self, chip, half):
        return {
            "scene": chip // (self.rows * self.pairs),
            "row": lax.rem(chip // self.pairs, self.rows),
            "col": lax.rem(chip, self.pairs) * 2 + half,
        }

    def beside(self, dr, dc):
        return {"scene": self.scene, "row": self.row + dr, "col": self.col + dc}

    def row_across(self, step):
        span = 2**step
        return self.row + span - 2 * span * lax.rem(self.row // span, 2)

    def plane_before(self, u):
        return lax.rem(self.plane + 2 * self.m - 1 - u, self.m)


def loop(low, high, body, unroll=1):
    def wrapped(j, carry):
        body(j)
        return carry

    lax.fori_loop(low, high, wrapped, 0, unroll=unroll)


def wait_all(ref, sem):
    pltpu.make_async_copy(ref, ref, sem).wait()


def inside(place, dr, dc):
    row, col = place.row + dr, place.col + dc
    fits = jnp.logical_and(row >= 0, row < place.rows)
    return jnp.logical_and(fits, jnp.logical_and(col >= 0, col < place.cols))


def greeted(place, dr, dc):
    if dc:
        return inside(place, dr, dc)
    first = place.row_across(0) if place.doublings else place.row
    return jnp.logical_and(inside(place, dr, dc), first != place.row + dr)


def greet(place):
    barrier = pltpu.get_barrier_semaphore()

    def signal(device):
        pl.semaphore_signal(barrier, inc=1, device_id=device, device_id_type=MESH)

    signal(place.device(place.me, 1 - place.half))
    for dr in (-1, 1):
        for dc in (-1, 0, 1):

            @pl.when(greeted(place, dr, dc))
            def _():
                signal(place.beside(dr, dc))

    def plane_peer(u):
        chip = place.chip(place.plane_after(u), place.row)
        signal(place.device(chip, place.half))
        signal(place.device(chip, 1 - place.half))

    loop(0, place.m - 1, plane_peer)
    for step in range(place.doublings):
        signal(place.device(place.chip(place.plane, place.row_across(step)), place.half))
    expected = jnp.int32(2 * place.m - 1 + place.doublings)
    for dr in (-1, 1):
        for dc in (-1, 0, 1):
            expected = expected + greeted(place, dr, dc).astype(jnp.int32)
    return barrier, expected


AROUND = tuple((dr, dc) for dr in (-1, 0, 1) for dc in (-1, 0, 1) if dr or dc)


def edge_of(dr, dc):
    if dr:
        return 1 if dr < 0 else 0
    return 3 if dc < 0 else 2


def halo_copies(place, edges, halo, halo_send, halo_recv):
    copies = []
    for slot, (dr, dc) in enumerate(AROUND):
        src, dst = edges.at[edge_of(dr, dc)], halo.at[slot]
        if dr and dc:
            width = edges.shape[2]
            part = pl.ds(width - 16, 16) if dc < 0 else pl.ds(0, 16)
            src, dst = src.at[:, part], dst.at[:, part]
        copy = pltpu.make_async_remote_copy(
            src_ref=src,
            dst_ref=dst,
            send_sem=halo_send.at[slot],
            recv_sem=halo_recv.at[slot],
            device_id=place.beside(-dr, -dc),
            device_id_type=MESH,
        )
        copies.append((copy, inside(place, -dr, -dc), inside(place, dr, dc)))
    return copies


def fill(place, which, cells, halo, cat, cols):
    height, width, channels = cells.shape

    def arrived(dr, dc):
        block = halo[AROUND.index((dr, dc)), which].astype(jnp.float32)
        return jnp.where(inside(place, dr, dc), block, 0.0)

    position = lax.broadcasted_iota(jnp.int32, (width, channels), 0)

    def put(r, line, left, right):
        before = jnp.where(position == 0, left, pltpu.roll(line, 1, 0))
        behind = jnp.where(position == width - 1, right, pltpu.roll(line, width - 1, 0))
        cat[r, :, 0:channels] = before.astype(cat.dtype)
        cat[r, :, channels : 2 * channels] = line.astype(cat.dtype)
        cat[r, :, 2 * channels : 3 * channels] = behind.astype(cat.dtype)

    cols[0] = arrived(0, -1)
    cols[1] = arrived(0, 1)
    for dr, r in ((-1, 0), (1, height + 1)):
        put(r, arrived(dr, 0), arrived(dr, -1)[width - 1 : width], arrived(dr, 1)[0:1])

    def inner(r):
        put(r + 1, cells[r].astype(jnp.float32), cols[0, pl.ds(r, 1), :], cols[1, pl.ds(r, 1), :])

    loop(0, height, inner, unroll=4)


def row_pairs(cat, layer, start, pairs):
    width, channels = cat.shape[2:]
    return jnp.concatenate(
        [jnp.concatenate([cat[layer, start + 2 * p + a] for p in range(pairs)], axis=0) for a in range(4)], axis=1
    )


def kernel(sizes, block_rows, data, params, scenes_hbm, cotangent_hbm, out,
           scenes, cotangent, edges, halo, cat, cols, flat, weights, outs, across, local,
           own, square, squares,
           theirs, sums, landed, kept, run, line_in, line_out,
           whole_own, whole_other, params_own, params_other,
           theirs_b, sums_b, landed_b, kept_b, passed_b, reached_b,
           load_sem, halo_send, halo_recv,
           swap_send, swap_recv, plane_send, plane_recv, line_send, line_recv,
           sq_send, sq_recv, gather_send, gather_recv, relay_send, relay_recv,
           pass_send, pass_recv, params_send, params_recv, carry_send, carry_recv,
           swap_send_b, swap_recv_b, plane_send_b, plane_recv_b, row_send_b, row_recv_b):
    place = Place(sizes)
    n, m, lines, me, half = place.n, place.m, place.rows, place.me, place.half
    height, width, channels = scenes.shape
    rows = params.shape[0]
    taps = 9
    full, half_type = jnp.float32, jnp.bfloat16
    partner = place.device(me, 1 - half)

    def remote(src, dst, send_sem, recv_sem, device):
        return pltpu.make_async_remote_copy(
            src_ref=src, dst_ref=dst, send_sem=send_sem, recv_sem=recv_sem,
            device_id=device, device_id_type=MESH,
        )

    def plane_device(u, to_half):
        return place.device(place.chip(place.plane_after(u), place.row), to_half)

    loads = [
        pltpu.make_async_copy(scenes_hbm, scenes, load_sem.at[0]),
        pltpu.make_async_copy(cotangent_hbm, cotangent, load_sem.at[1]),
    ]

    load_own = pltpu.make_async_copy(data.at[:, :, :, half], own, load_sem.at[3])
    barrier, expected = greet(place)
    load_params = pltpu.make_async_copy(params, params_own.at[place.row, place.plane], load_sem.at[2])
    load_params.start()
    load_own.start()
    for load in loads:
        load.start()
    for layer in range(2):
        weights[layer, 9 * channels : 12 * channels, 0:channels] = jnp.zeros((3 * channels, channels), half_type)
        weights[layer, 0 : 3 * channels, channels : 2 * channels] = jnp.zeros((3 * channels, channels), half_type)
    pl.semaphore_wait(barrier, expected)

    def swap(t):
        return remote(data.at[:, t, :, 1 - half], theirs.at[t], swap_send, swap_recv.at[t], partner)

    loop(0, lines, lambda t: swap(t).start())

    def row_device(step):
        return place.device(place.chip(place.plane, place.row_across(step)), half)

    def passing(step, row):
        block = params_own.at[row, place.plane]
        return remote(block, block, pass_send, pass_recv.at[step], row_device(step))

    load_params.wait()
    for step in range(place.doublings):
        passing(step, place.row).start()

    def others(step):
        span = 2**step
        first = place.row // span * span
        return [first + lax.rem(place.row - first + k, span) for k in range(1, span)]

    def pass_on_params(step):
        for row in others(step):
            passing(step, row).start()

    def params_come(step):
        wait_all(params_own.at[pl.ds(0, 2**step), 0], pass_recv.at[step])

    load_own.wait()

    def both(t, plane):
        scene, pair = plane // place.pairs, lax.rem(plane, place.pairs)
        return own[scene, t, pair] + theirs[t, scene, pair]

    def across_plane(t):
        swap(t).wait_recv()

        def pass_on(u):
            slot = t * (m - 1) + u
            sums[slot] = both(t, place.plane_after(u)).astype(sums.dtype)
            remote(sums.at[slot], landed.at[t, u], plane_send, plane_recv.at[t], plane_device(u, half)).start()

        loop(0, m - 1, pass_on)
        kept[t] = both(t, place.plane)

    loop(0, lines, across_plane)

    for which, (load, cells) in enumerate(zip(loads, (scenes, cotangent))):
        load.wait()
        edges[0, which] = cells[0]
        edges[1, which] = cells[height - 1]
        edges[2, which] = cells[:, 0:16, :].astype(full)[:, 0, :].astype(edges.dtype)
        edges[3, which] = cells[:, width - 16 : width, :].astype(full)[:, 15, :].astype(edges.dtype)
    halos = halo_copies(place, edges, halo, halo_send, halo_recv)
    for copy, out_of, into in halos:
        pl.when(out_of)(copy.start)

    def along(step, t):
        return remote(line_out.at[step, t], line_in.at[step, t], line_send, line_recv.at[step, t], row_device(step))

    side = me // (n // 2)
    near_count = m // 2

    def towards(k, sign):
        near = side * near_count + lax.rem(place.plane + near_count * 2 + sign * (k + 1), near_count)
        far = (1 - side) * near_count + lax.rem(place.plane + near_count * 2 + sign * k, near_count)
        return near, far

    def give(plane, slot, t):
        mine = whole_own.at[t, place.plane]
        device = place.device(place.chip(plane, place.row), half)
        return remote(mine, mine, gather_send, gather_recv.at[t, slot], device)

    def relay(t, plane, far):
        return remote(whole_own.at[t, plane], whole_other.at[t, plane], relay_send, relay_recv.at[far], partner)

    def give_near(t):
        loop(0, near_count - 1, lambda k: give(towards(k, 1)[0], k, t).start())

    def give_far(i):
        t, k = i // near_count, lax.rem(i, near_count)
        give(towards(k, 1)[1], near_count - 1 + k, t).start()

    def give_params(row):
        block = params_own.at[row, place.plane]

        def to(plane, far):
            device = place.device(place.chip(plane, place.row), half)
            remote(block, block, params_send, params_recv.at[far], device).start()

        loop(0, near_count - 1, lambda k: to(towards(k, 1)[0], 0))
        loop(0, near_count, lambda k: to(towards(k, 1)[1], 1))

    def carry(far):
        first = jnp.where(far == 1, 1 - side, side) * near_count
        planes = pl.ds(first, near_count)
        return remote(params_own.at[:, planes], params_other.at[:, planes], carry_send, carry_recv.at[far], partner)

    def share(step, t, total):
        run[t] = total
        if step < place.doublings:
            line_out[step, t] = total.astype(half_type)
            along(step, t).start()
        else:
            whole_own[t, place.plane] = total.astype(half_type)
            give_near(t)
            relay(t, place.plane, 0).start()

    def plane_sum(t):
        wait_all(landed.at[t], plane_recv.at[t])
        share(0, t, lax.fori_loop(0, m - 1, lambda u, sofar: sofar + landed[t, u].astype(full), kept[t]))

    def line_sum(step, t):
        along(step, t).wait_recv()
        share(step + 1, t, run[t] + line_in[step, t].astype(full))

    give_params(place.row)
    if place.doublings:
        params_come(0)
        give_params(place.row_across(0))
    if place.doublings > 1:
        pass_on_params(1)
    def more_params(step):
        if step > 1:
            pass_on_params(step)
        params_come(step)
        first = place.row_across(step) // 2**step * 2**step
        for k in range(2**step):
            give_params(first + k)

    loop(0, lines, plane_sum)
    if place.doublings > 1:
        more_params(1)
    if place.doublings:
        loop(0, lines, functools.partial(line_sum, 0))
    for step in range(2, place.doublings):
        more_params(step)
    for copy, out_of, into in halos:
        pl.when(into)(copy.wait_recv)
    fill(place, 0, scenes, halo, cat.at[0], cols)
    fill(place, 1, cotangent, halo, cat.at[1], cols)
    for step in range(1, place.doublings):
        loop(0, lines, functools.partial(line_sum, step))
    square[0] = jnp.sum(lax.fori_loop(0, lines, lambda t, sofar: sofar + run[t] * run[t], jnp.zeros((rows, LANES), full)), axis=0, keepdims=True)

    def arrive(t, plane, slot, far):
        there = whole_own.at[t, plane]
        remote(there, there, gather_send, gather_recv.at[t, slot], partner).wait_recv()
        relay(t, plane, far).start()

    def from_near(i):
        t, k = i // (near_count - 1), lax.rem(i, near_count - 1)
        arrive(t, towards(k, -1)[0], k, 0)

    def from_far(i):
        t, k = i // near_count, lax.rem(i, near_count)
        arrive(t, towards(k, -1)[1], near_count - 1 + k, 1)

    def tell(device, slot):
        return remote(square.at[0], squares.at[slot], sq_send, sq_recv, device)

    def tell_chip(u):
        tell(plane_device(u, half), 2 * u + 1).start()
        tell(plane_device(u, 1 - half), 2 * u + 2).start()

    loop(0, m - 1, tell_chip)
    tell(partner, 0).start()
    loop(0, lines * near_count, give_far)
    wait_all(params_own.at[:, pl.ds(0, near_count - 1)], params_recv.at[0])
    carry(0).start()
    wait_all(params_own.at[:, pl.ds(0, near_count)], params_recv.at[1])
    carry(1).start()
    loop(0, lines * (near_count - 1), from_near)
    wait_all(squares, sq_recv)
    norm2 = jnp.sum(square[0] + jnp.sum(squares[...], axis=0))
    factor = radius / (jnp.sqrt(jnp.full((1, LANES), norm2, full)) + epsilon)

    def spread(layer, i):
        t, plane = i // near_count, layer * near_count + lax.rem(i, near_count)
        c = 2 * place.chip(plane, t)
        flat[pl.ds((c + half) * rows, rows), :] = params_own[t, plane] + factor * whole_own[t, plane].astype(full)
        flat[pl.ds((c + 1 - half) * rows, rows), :] = params_other[t, plane] + factor * whole_other[t, plane].astype(full)

    def put(layer, t, kernel):
        weights[layer, t * channels : (t + 1) * channels, 0:channels] = kernel
        weights[layer, (t + 3) * channels : (t + 4) * channels, channels : 2 * channels] = kernel

    def weigh(layer):
        far = jnp.where(layer == side, 0, 1)
        wait_all(params_other.at[:, pl.ds(0, near_count)], carry_recv.at[far])
        wait_all(whole_other.at[:, pl.ds(0, near_count)], relay_recv.at[far])
        loop(0, lines * near_count, functools.partial(spread, layer), unroll=4)

        @pl.when(layer == 0)
        def _():
            for t in range(taps):
                put(0, t, flat[t * channels : (t + 1) * channels].astype(half_type))

        @pl.when(layer == 1)
        def _():
            for t in range(taps):
                first = (2 * taps - 1 - t) * channels
                put(1, t, flat[first : first + channels].T.astype(half_type))

    blocks, pairs = height // block_rows, block_rows // 2

    def convolve(layer, i):
        start = i * block_rows
        pair = jnp.dot(row_pairs(cat, layer, start, pairs), weights[layer], preferred_element_type=full)
        both_rows = []
        for p in range(pairs):
            part = pair[p * width : (p + 1) * width]
            both_rows.append(jnp.concatenate([part[:, 0:channels], part[:, channels:]], axis=0))
        return start, both_rows

    def convolve_near(i):
        start, both_rows = convolve(side, i)
        for p, cells in enumerate(both_rows):
            outs[pl.ds(start + 2 * p, 2)] = cells.reshape(2, width, channels)

    def convolve_far(i):
        start, both_rows = convolve(1 - side, i)
        for p, cells in enumerate(both_rows):
            near = outs[pl.ds(start + 2 * p, 2)].reshape(2 * width, channels)
            pre = jnp.where(side == 0, near, cells)
            back = jnp.where(side == 0, cells, near)
            squash = jax.nn.sigmoid(pre)
            at = pl.ds(pl.multiple_of((start + 2 * p) * width, 2 * width), 2 * width)
            across[0, :, at] = (back * squash * (1.0 + pre * (1.0 - squash))).T.astype(half_type)
            across[1, :, at] = (pre * squash).T.astype(half_type)

    def take_far():
        loop(0, lines * near_count, from_far)

    pl.when(half == 1)(take_far)
    weigh(side)
    def near_block(i):
        pl.when(jnp.logical_and(i == blocks // 2, half == 0))(take_far)
        convolve_near(i)

    loop(0, blocks, near_block)
    weigh(1 - side)
    loop(0, blocks, convolve_far)

    def field_grad(group, layers=(0, 1)):
        for layer in layers:
            field = jnp.concatenate([
                cat[layer, u // 3 : u // 3 + height, :, u % 3 * channels : (u % 3 + 1) * channels].reshape(height * width, channels)
                for u in group
            ], axis=1)
            grad = jnp.dot(across[layer], field, preferred_element_type=full)
            for i, u in enumerate(group):
                tap = grad[:, i * channels : (i + 1) * channels]
                if layer == 0:
                    flat[u * channels : (u + 1) * channels] = tap.T
                else:
                    t = 2 * taps - 1 - u
                    flat[t * channels : (t + 1) * channels] = tap

    def ready(i, c):
        for h in range(2):
            local[c, h] = flat[pl.ds((2 * c + h) * rows, rows), :]
        remote(local.at[c, 1 - half], theirs_b.at[c], swap_send_b, swap_recv_b.at[i], partner).start()

    def pass_b(c):
        plane = c // (lines * place.pairs) * place.pairs + lax.rem(c, place.pairs)
        row = lax.rem(c // place.pairs, lines)
        total = local[c, half] + theirs_b[c]

        @pl.when(plane == place.plane)
        def _():
            kept_b[row] = total

        @pl.when(plane != place.plane)
        def _():
            u = lax.rem(plane - place.plane - 1 + m, m)
            sums_b[c] = total.astype(half_type)
            remote(sums_b.at[c], landed_b.at[row, u], plane_send_b, plane_recv_b.at[row], plane_device(u, half)).start()

    def completed_by(c):
        touched = range(2 * c * rows // channels, (2 * (c + 1) * rows - 1) // channels + 1)
        return max(i for i, group in enumerate(TAP_GROUPS) if any(t in group for t in touched))

    def each_chunk(chunks, body):
        def mirrored(c):
            body(c)
            body(n - 1 - c)

        starts = [c for c in chunks if c - 1 not in chunks]
        ends = [c + 1 for c in chunks if c + 1 not in chunks]
        for low, high in zip(starts, ends):
            loop(low, high, mirrored)

    completed = [[c for c in range(n // 2) if completed_by(c) == i] for i in range(len(TAP_GROUPS))]

    def pass_group(i):
        wait_all(theirs_b.at[pl.ds(0, 2 * len(completed[i]))], swap_recv_b.at[i])
        each_chunk(completed[i], pass_b)

    for i, group in enumerate(TAP_GROUPS):
        field_grad(group)
        each_chunk(completed[i], functools.partial(ready, i))
        if i:
            pass_group(i - 1)
    pass_group(len(TAP_GROUPS) - 1)

    def along_rows(k):
        row = jnp.where(side == 0, k, lines - 1 - k)
        wait_all(landed_b.at[row], plane_recv_b.at[row])
        total = lax.fori_loop(0, m - 1, lambda u, sofar: sofar + landed_b[row, u].astype(full), kept_b[row])
        kept_b[row] = total

        @pl.when(row != place.row)
        def _():
            t = lax.rem(row - place.row - 1 + lines, lines)
            passed_b[t] = total.astype(half_type)
            device = place.device(place.chip(place.plane, row), half)
            remote(passed_b.at[t], reached_b.at[t], row_send_b, row_recv_b, device).start()

    loop(0, lines, along_rows)
    wait_all(theirs, swap_send)
    wait_all(sums, plane_send)
    wait_all(squares, sq_send)
    wait_all(whole_other, relay_send)
    wait_all(params_own.at[pl.ds(0, lines - 1), 0], pass_send)
    wait_all(params_own.at[:, pl.ds(0, m - 1)], params_send)
    wait_all(params_own, carry_send)
    wait_all(whole_own.at[:, pl.ds(0, m - 1)], gather_send)
    for copy, out_of, into in halos:
        pl.when(out_of)(copy.wait_send)
    if place.doublings:
        wait_all(line_out, line_send)
    wait_all(theirs_b, swap_send_b)
    wait_all(sums_b.at[pl.ds(0, n - lines)], plane_send_b)
    wait_all(reached_b, row_recv_b)
    out[...] = lax.fori_loop(0, lines - 1, lambda t, sofar: sofar + reached_b[t].astype(full), kept_b[place.row])
    wait_all(reached_b, row_send_b)


def on_device(sizes, scenes, cotangent, params, partials):
    scenes, cotangent = scenes[0], cotangent[0]
    height, width, channels = scenes.shape
    n = sizes[0] * sizes[1] * sizes[2] // 2
    rows = params.size // LANES
    dma = pltpu.SemaphoreType.DMA
    half_type, full = jnp.bfloat16, jnp.float32
    anywhere, vmem = pl.BlockSpec(memory_space=pl.ANY), pl.BlockSpec(memory_space=pltpu.VMEM)
    lines, m = sizes[1], n // sizes[1]
    one = (rows, LANES)
    doublings = max((lines - 1).bit_length(), 1)
    scratch = [
        pltpu.VMEM(scenes.shape, half_type),
        pltpu.VMEM(scenes.shape, half_type),
        pltpu.VMEM((4, 2, width, channels), half_type),
        pltpu.VMEM((len(AROUND), 2, width, channels), half_type),
        pltpu.VMEM((2, height + 2, width, 3 * channels), half_type),
        pltpu.VMEM((2, height, channels), full),
        pltpu.VMEM((18 * channels, channels), full),
        pltpu.VMEM((2, 12 * channels, 2 * channels), half_type),
        pltpu.VMEM((height, width, channels), full),
        pltpu.VMEM((2, channels, height * width), half_type),
        pltpu.VMEM((n, 2, *one), full),
        pltpu.VMEM((sizes[0], lines, sizes[2] // 2, *one), full),
        pltpu.VMEM((1, 1, LANES), full),
        pltpu.VMEM((2 * m - 1, 1, LANES), full),
        pltpu.VMEM((lines, sizes[0], sizes[2] // 2, *one), full),
        pltpu.VMEM((n - lines, *one), half_type),
        pltpu.VMEM((lines, m - 1, *one), half_type),
        pltpu.VMEM((lines, *one), full),
        pltpu.VMEM((lines, *one), full),
        pltpu.VMEM((doublings, lines, *one), half_type),
        pltpu.VMEM((doublings, lines, *one), half_type),
        pltpu.VMEM((lines, m, *one), half_type),
        pltpu.VMEM((lines, m, *one), half_type),
        pltpu.VMEM((lines, m, *one), full),
        pltpu.VMEM((lines, m, *one), full),
        pltpu.VMEM((n, *one), full),
        pltpu.VMEM((n, *one), half_type),
        pltpu.VMEM((lines, m - 1, *one), half_type),
        pltpu.VMEM((lines, *one), full),
        pltpu.VMEM((lines - 1, *one), half_type),
        pltpu.VMEM((lines - 1, *one), half_type),
        dma((4,)), dma((len(AROUND),)), dma((len(AROUND),)),
        dma, dma((lines,)), dma, dma((lines,)), dma, dma((doublings, lines)),
        dma, dma, dma, dma((lines, m - 1)), dma, dma((2,)),
        dma, dma((doublings,)), dma, dma((2,)), dma, dma((2,)),
        dma, dma((len(TAP_GROUPS),)), dma, dma((lines,)), dma, dma,
    ]
    grads = pl.pallas_call(
        functools.partial(kernel, sizes, 32),
        out_shape=pltpu.VMEM((rows, LANES), full),
        in_specs=[anywhere, anywhere, anywhere, anywhere],
        out_specs=vmem,
        scratch_shapes=scratch,
        compiler_params=pltpu.CompilerParams(
            collective_id=0, has_side_effects=True, vmem_limit_bytes=56 * 2**20
        ),
        name="sam_grad",
    )(partials[0].reshape(sizes[0], lines, sizes[2] // 2, 2, rows, LANES), params.reshape(rows, LANES), scenes, cotangent)
    return grads.reshape(-1)


def solution(mesh):
    sizes = tuple(mesh.shape[axis] for axis in AXES)
    return jax.shard_map(
        functools.partial(on_device, sizes),
        mesh=mesh,
        in_specs=(
            P("scene", "row", "col", None),
            P("scene", "row", "col", None),
            P(AXES),
            P(AXES, None),
        ),
        out_specs=P(AXES),
        check_vma=False,
    )
```

```python
import functools

import jax
import jax.numpy as jnp
from jax import lax
from jax.experimental import pallas as pl
from jax.experimental.pallas import tpu as pltpu
from jax.sharding import PartitionSpec as P

radius = 2.0
epsilon = 1e-06
AXES = ("scene", "row", "col")
MESH = pl.DeviceIdType.MESH
LANES = 128
TAP_GROUPS = ((0, 1, 4, 5), (2, 3, 6, 7), (8,))


class Place:
    def __init__(self, sizes):
        self.scenes, self.rows, self.cols = sizes
        self.pairs = self.cols // 2
        self.n = self.scenes * self.rows * self.pairs
        self.col = col = lax.axis_index("col")
        self.scene = lax.axis_index("scene")
        self.half = lax.rem(col, 2)
        self.m = self.scenes * self.pairs
        self.doublings = (self.rows - 1).bit_length()
        self.row = lax.axis_index("row")
        self.plane = lax.axis_index("scene") * self.pairs + col // 2
        self.me = self.chip(self.plane, self.row)

    def chip(self, plane, row):
        return (plane // self.pairs * self.rows + row) * self.pairs + lax.rem(plane, self.pairs)

    def plane_after(self, u):
        return lax.rem(self.plane + 1 + u, self.m)

    def row_after(self, t):
        return lax.rem(self.row + 1 + t, self.rows)

    def order(self, j):
        return self.chip(self.plane_after(lax.rem(j, self.m)), self.row_after(j // self.m))

    def device(self, chip, half):
        return {
            "scene": chip // (self.rows * self.pairs),
            "row": lax.rem(chip // self.pairs, self.rows),
            "col": lax.rem(chip, self.pairs) * 2 + half,
        }

    def beside(self, dr, dc):
        return {"scene": self.scene, "row": self.row + dr, "col": self.col + dc}

    def row_across(self, step):
        span = 2**step
        return self.row + span - 2 * span * lax.rem(self.row // span, 2)

    def plane_before(self, u):
        return lax.rem(self.plane + 2 * self.m - 1 - u, self.m)


def loop(low, high, body, unroll=1):
    def wrapped(j, carry):
        body(j)
        return carry

    lax.fori_loop(low, high, wrapped, 0, unroll=unroll)


def wait_all(ref, sem):
    pltpu.make_async_copy(ref, ref, sem).wait()


def inside(place, dr, dc):
    row, col = place.row + dr, place.col + dc
    fits = jnp.logical_and(row >= 0, row < place.rows)
    return jnp.logical_and(fits, jnp.logical_and(col >= 0, col < place.cols))


def greeted(place, dr, dc):
    if dc:
        return inside(place, dr, dc)
    first = place.row_across(0) if place.doublings else place.row
    return jnp.logical_and(inside(place, dr, dc), first != place.row + dr)


def greet(place):
    barrier = pltpu.get_barrier_semaphore()

    def signal(device):
        pl.semaphore_signal(barrier, inc=1, device_id=device, device_id_type=MESH)

    signal(place.device(place.me, 1 - place.half))
    for dr in (-1, 1):
        for dc in (-1, 0, 1):

            @pl.when(greeted(place, dr, dc))
            def _():
                signal(place.beside(dr, dc))

    def plane_peer(u):
        chip = place.chip(place.plane_after(u), place.row)
        signal(place.device(chip, place.half))
        signal(place.device(chip, 1 - place.half))

    loop(0, place.m - 1, plane_peer)
    for step in range(place.doublings):
        signal(place.device(place.chip(place.plane, place.row_across(step)), place.half))
    expected = jnp.int32(2 * place.m - 1 + place.doublings)
    for dr in (-1, 1):
        for dc in (-1, 0, 1):
            expected = expected + greeted(place, dr, dc).astype(jnp.int32)
    return barrier, expected


AROUND = tuple((dr, dc) for dr in (-1, 0, 1) for dc in (-1, 0, 1) if dr or dc)


def edge_of(dr, dc):
    if dr:
        return 1 if dr < 0 else 0
    return 3 if dc < 0 else 2


def halo_copies(place, edges, halo, halo_send, halo_recv):
    copies = []
    for slot, (dr, dc) in enumerate(AROUND):
        src, dst = edges.at[edge_of(dr, dc)], halo.at[slot]
        if dr and dc:
            width = edges.shape[2]
            part = pl.ds(width - 16, 16) if dc < 0 else pl.ds(0, 16)
            src, dst = src.at[:, part], dst.at[:, part]
        copy = pltpu.make_async_remote_copy(
            src_ref=src,
            dst_ref=dst,
            send_sem=halo_send.at[slot],
            recv_sem=halo_recv.at[slot],
            device_id=place.beside(-dr, -dc),
            device_id_type=MESH,
        )
        copies.append((copy, inside(place, -dr, -dc), inside(place, dr, dc)))
    return copies


def fill(place, which, cells, halo, cat, cols):
    height, width, channels = cells.shape

    def arrived(dr, dc):
        block = halo[AROUND.index((dr, dc)), which].astype(jnp.float32)
        return jnp.where(inside(place, dr, dc), block, 0.0)

    position = lax.broadcasted_iota(jnp.int32, (width, channels), 0)

    def put(r, line, left, right):
        before = jnp.where(position == 0, left, pltpu.roll(line, 1, 0))
        behind = jnp.where(position == width - 1, right, pltpu.roll(line, width - 1, 0))
        cat[r, :, 0:channels] = before.astype(cat.dtype)
        cat[r, :, channels : 2 * channels] = line.astype(cat.dtype)
        cat[r, :, 2 * channels : 3 * channels] = behind.astype(cat.dtype)

    cols[0] = arrived(0, -1)
    cols[1] = arrived(0, 1)
    for dr, r in ((-1, 0), (1, height + 1)):
        put(r, arrived(dr, 0), arrived(dr, -1)[width - 1 : width], arrived(dr, 1)[0:1])

    def inner(r):
        put(r + 1, cells[r].astype(jnp.float32), cols[0, pl.ds(r, 1), :], cols[1, pl.ds(r, 1), :])

    loop(0, height, inner, unroll=4)


def row_pairs(cat, layer, start, pairs):
    width, channels = cat.shape[2:]
    return jnp.concatenate(
        [jnp.concatenate([cat[layer, start + 2 * p + a] for p in range(pairs)], axis=0) for a in range(4)], axis=1
    )


def kernel(sizes, block_rows, data, params, scenes_hbm, cotangent_hbm, out,
           scenes, cotangent, edges, halo, cat, cols, flat, weights, outs, across, local,
           own, square, squares,
           theirs, sums, landed, kept, run, line_in, line_out,
           whole_own, whole_other, params_own, params_other,
           theirs_b, sums_b, landed_b, kept_b, passed_b, reached_b,
           load_sem, halo_send, halo_recv,
           swap_send, swap_recv, plane_send, plane_recv, line_send, line_recv,
           sq_send, sq_recv, gather_send, gather_recv, relay_send, relay_recv,
           pass_send, pass_recv, params_send, params_recv, carry_send, carry_recv,
           swap_send_b, swap_recv_b, plane_send_b, plane_recv_b, row_send_b, row_recv_b):
    place = Place(sizes)
    n, m, lines, me, half = place.n, place.m, place.rows, place.me, place.half
    height, width, channels = scenes.shape
    rows = params.shape[0]
    taps = 9
    full, half_type = jnp.float32, jnp.bfloat16
    partner = place.device(me, 1 - half)

    def remote(src, dst, send_sem, recv_sem, device):
        return pltpu.make_async_remote_copy(
            src_ref=src, dst_ref=dst, send_sem=send_sem, recv_sem=recv_sem,
            device_id=device, device_id_type=MESH,
        )

    def plane_device(u, to_half):
        return place.device(place.chip(place.plane_after(u), place.row), to_half)

    loads = [
        pltpu.make_async_copy(scenes_hbm, scenes, load_sem.at[0]),
        pltpu.make_async_copy(cotangent_hbm, cotangent, load_sem.at[1]),
    ]

    load_own = pltpu.make_async_copy(data.at[:, :, :, half], own, load_sem.at[3])
    barrier, expected = greet(place)
    load_params = pltpu.make_async_copy(params, params_own.at[place.row, place.plane], load_sem.at[2])
    load_params.start()
    load_own.start()
    for load in loads:
        load.start()
    for layer in range(2):
        weights[layer, 9 * channels : 12 * channels, 0:channels] = jnp.zeros((3 * channels, channels), half_type)
        weights[layer, 0 : 3 * channels, channels : 2 * channels] = jnp.zeros((3 * channels, channels), half_type)
    pl.semaphore_wait(barrier, expected)

    def swap(t):
        return remote(data.at[:, t, :, 1 - half], theirs.at[t], swap_send, swap_recv.at[t], partner)

    loop(0, lines, lambda t: swap(t).start())

    def row_device(step):
        return place.device(place.chip(place.plane, place.row_across(step)), half)

    def passing(step, row):
        block = params_own.at[row, place.plane]
        return remote(block, block, pass_send, pass_recv.at[step], row_device(step))

    load_params.wait()
    for step in range(place.doublings):
        passing(step, place.row).start()

    def others(step):
        span = 2**step
        first = place.row // span * span
        return [first + lax.rem(place.row - first + k, span) for k in range(1, span)]

    def pass_on_params(step):
        for row in others(step):
            passing(step, row).start()

    def params_come(step):
        wait_all(params_own.at[pl.ds(0, 2**step), 0], pass_recv.at[step])

    load_own.wait()

    def both(t, plane):
        scene, pair = plane // place.pairs, lax.rem(plane, place.pairs)
        return own[scene, t, pair] + theirs[t, scene, pair]

    def across_plane(t):
        swap(t).wait_recv()

        def pass_on(u):
            slot = t * (m - 1) + u
            sums[slot] = both(t, place.plane_after(u)).astype(sums.dtype)
            remote(sums.at[slot], landed.at[t, u], plane_send, plane_recv.at[t], plane_device(u, half)).start()

        loop(0, m - 1, pass_on)
        kept[t] = both(t, place.plane)

    loop(0, lines, across_plane)

    for which, (load, cells) in enumerate(zip(loads, (scenes, cotangent))):
        load.wait()
        edges[0, which] = cells[0]
        edges[1, which] = cells[height - 1]
        edges[2, which] = cells[:, 0:16, :].astype(full)[:, 0, :].astype(edges.dtype)
        edges[3, which] = cells[:, width - 16 : width, :].astype(full)[:, 15, :].astype(edges.dtype)
    halos = halo_copies(place, edges, halo, halo_send, halo_recv)
    for copy, out_of, into in halos:
        pl.when(out_of)(copy.start)

    def along(step, t):
        return remote(line_out.at[step, t], line_in.at[step, t], line_send, line_recv.at[step, t], row_device(step))

    side = me // (n // 2)
    near_count = m // 2

    def towards(k, sign):
        near = side * near_count + lax.rem(place.plane + near_count * 2 + sign * (k + 1), near_count)
        far = (1 - side) * near_count + lax.rem(place.plane + near_count * 2 + sign * k, near_count)
        return near, far

    def give(plane, slot, t):
        mine = whole_own.at[t, place.plane]
        device = place.device(place.chip(plane, place.row), half)
        return remote(mine, mine, gather_send, gather_recv.at[t, slot], device)

    def relay(t, plane, far):
        return remote(whole_own.at[t, plane], whole_other.at[t, plane], relay_send, relay_recv.at[far], partner)

    def give_near(t):
        loop(0, near_count - 1, lambda k: give(towards(k, 1)[0], k, t).start())

    def give_far(i):
        t, k = i // near_count, lax.rem(i, near_count)
        give(towards(k, 1)[1], near_count - 1 + k, t).start()

    def give_params(row):
        block = params_own.at[row, place.plane]

        def to(plane, far):
            device = place.device(place.chip(plane, place.row), half)
            remote(block, block, params_send, params_recv.at[far], device).start()

        loop(0, near_count - 1, lambda k: to(towards(k, 1)[0], 0))
        loop(0, near_count, lambda k: to(towards(k, 1)[1], 1))

    def carry(far):
        first = jnp.where(far == 1, 1 - side, side) * near_count
        planes = pl.ds(first, near_count)
        return remote(params_own.at[:, planes], params_other.at[:, planes], carry_send, carry_recv.at[far], partner)

    def tell(device, slot):
        return remote(square.at[0], squares.at[slot], sq_send, sq_recv, device)

    def tell_chip(u):
        tell(plane_device(u, half), 2 * u + 1).start()
        tell(plane_device(u, 1 - half), 2 * u + 2).start()

    def tell_all():
        norm2 = lax.fori_loop(0, lines, lambda t, sofar: sofar + run[t] * run[t], jnp.zeros((rows, LANES), full))
        square[0] = jnp.sum(norm2, axis=0, keepdims=True)
        loop(0, m - 1, tell_chip)
        tell(partner, 0).start()

    def share(step, t, total):
        run[t] = total
        if step < place.doublings:
            line_out[step, t] = total.astype(half_type)
            along(step, t).start()
        else:
            whole_own[t, place.plane] = total.astype(half_type)
            pl.when(t == lines - 1)(tell_all)
            give_near(t)
            relay(t, place.plane, 0).start()

    def plane_sum(t):
        wait_all(landed.at[t], plane_recv.at[t])
        share(0, t, lax.fori_loop(0, m - 1, lambda u, sofar: sofar + landed[t, u].astype(full), kept[t]))

    def line_sum(step, t):
        along(step, t).wait_recv()
        share(step + 1, t, run[t] + line_in[step, t].astype(full))

    give_params(place.row)
    if place.doublings:
        params_come(0)
        give_params(place.row_across(0))
    if place.doublings > 1:
        pass_on_params(1)
    def more_params(step):
        if step > 1:
            pass_on_params(step)
        params_come(step)
        first = place.row_across(step) // 2**step * 2**step
        for k in range(2**step):
            give_params(first + k)

    loop(0, lines, plane_sum)
    if place.doublings > 1:
        more_params(1)
    if place.doublings:
        loop(0, lines, functools.partial(line_sum, 0))
    for step in range(2, place.doublings):
        more_params(step)
    for copy, out_of, into in halos:
        pl.when(into)(copy.wait_recv)
    fill(place, 0, scenes, halo, cat.at[0], cols)
    for step in range(1, place.doublings):
        loop(0, lines, functools.partial(line_sum, step))
    def arrive(t, plane, slot, far):
        there = whole_own.at[t, plane]
        remote(there, there, gather_send, gather_recv.at[t, slot], partner).wait_recv()
        relay(t, plane, far).start()

    def from_near(i):
        t, k = i // (near_count - 1), lax.rem(i, near_count - 1)
        arrive(t, towards(k, -1)[0], k, 0)

    def from_far(i):
        t, k = i // near_count, lax.rem(i, near_count)
        arrive(t, towards(k, -1)[1], near_count - 1 + k, 1)

    loop(0, lines * near_count, give_far)
    fill(place, 1, cotangent, halo, cat.at[1], cols)
    wait_all(params_own.at[:, pl.ds(0, near_count - 1)], params_recv.at[0])
    carry(0).start()
    wait_all(params_own.at[:, pl.ds(0, near_count)], params_recv.at[1])
    carry(1).start()
    loop(0, lines * (near_count - 1), from_near)
    wait_all(squares, sq_recv)
    norm2 = jnp.sum(square[0] + jnp.sum(squares[...], axis=0))
    factor = radius / (jnp.sqrt(jnp.full((1, LANES), norm2, full)) + epsilon)

    def spread(layer, i):
        t, plane = i // near_count, layer * near_count + lax.rem(i, near_count)
        c = 2 * place.chip(plane, t)
        flat[pl.ds((c + half) * rows, rows), :] = params_own[t, plane] + factor * whole_own[t, plane].astype(full)
        flat[pl.ds((c + 1 - half) * rows, rows), :] = params_other[t, plane] + factor * whole_other[t, plane].astype(full)

    def put(layer, t, kernel):
        weights[layer, t * channels : (t + 1) * channels, 0:channels] = kernel
        weights[layer, (t + 3) * channels : (t + 4) * channels, channels : 2 * channels] = kernel

    def weigh(layer):
        far = jnp.where(layer == side, 0, 1)
        wait_all(params_other.at[:, pl.ds(0, near_count)], carry_recv.at[far])
        wait_all(whole_other.at[:, pl.ds(0, near_count)], relay_recv.at[far])
        loop(0, lines * near_count, functools.partial(spread, layer), unroll=4)

        @pl.when(layer == 0)
        def _():
            for t in range(taps):
                put(0, t, flat[t * channels : (t + 1) * channels].astype(half_type))

        @pl.when(layer == 1)
        def _():
            for t in range(taps):
                first = (2 * taps - 1 - t) * channels
                put(1, t, flat[first : first + channels].T.astype(half_type))

    blocks, pairs = height // block_rows, block_rows // 2

    def convolve(layer, i):
        start = i * block_rows
        pair = jnp.dot(row_pairs(cat, layer, start, pairs), weights[layer], preferred_element_type=full)
        both_rows = []
        for p in range(pairs):
            part = pair[p * width : (p + 1) * width]
            both_rows.append(jnp.concatenate([part[:, 0:channels], part[:, channels:]], axis=0))
        return start, both_rows

    def convolve_near(i):
        start, both_rows = convolve(side, i)
        for p, cells in enumerate(both_rows):
            outs[pl.ds(start + 2 * p, 2)] = cells.reshape(2, width, channels)

    def convolve_far(i):
        start, both_rows = convolve(1 - side, i)
        for p, cells in enumerate(both_rows):
            near = outs[pl.ds(start + 2 * p, 2)].reshape(2 * width, channels)
            pre = jnp.where(side == 0, near, cells)
            back = jnp.where(side == 0, cells, near)
            squash = jax.nn.sigmoid(pre)
            at = pl.ds(pl.multiple_of((start + 2 * p) * width, 2 * width), 2 * width)
            across[0, :, at] = (back * squash * (1.0 + pre * (1.0 - squash))).T.astype(half_type)
            across[1, :, at] = (pre * squash).T.astype(half_type)

    def take_far():
        loop(0, lines * near_count, from_far)

    pl.when(half == 1)(take_far)
    weigh(side)
    def near_block(i):
        pl.when(jnp.logical_and(i == blocks // 2, half == 0))(take_far)
        convolve_near(i)

    loop(0, blocks, near_block)
    weigh(1 - side)
    loop(0, blocks, convolve_far)

    def field_grad(group, layers=(0, 1)):
        for layer in layers:
            field = jnp.concatenate([
                cat[layer, u // 3 : u // 3 + height, :, u % 3 * channels : (u % 3 + 1) * channels].reshape(height * width, channels)
                for u in group
            ], axis=1)
            grad = jnp.dot(across[layer], field, preferred_element_type=full)
            for i, u in enumerate(group):
                tap = grad[:, i * channels : (i + 1) * channels]
                if layer == 0:
                    flat[u * channels : (u + 1) * channels] = tap.T
                else:
                    t = 2 * taps - 1 - u
                    flat[t * channels : (t + 1) * channels] = tap

    def ready(i, c):
        for h in range(2):
            local[c, h] = flat[pl.ds((2 * c + h) * rows, rows), :]
        remote(local.at[c, 1 - half], theirs_b.at[c], swap_send_b, swap_recv_b.at[i], partner).start()

    def pass_b(c):
        plane = c // (lines * place.pairs) * place.pairs + lax.rem(c, place.pairs)
        row = lax.rem(c // place.pairs, lines)
        total = local[c, half] + theirs_b[c]

        @pl.when(plane == place.plane)
        def _():
            kept_b[row] = total

        @pl.when(plane != place.plane)
        def _():
            u = lax.rem(plane - place.plane - 1 + m, m)
            sums_b[c] = total.astype(half_type)
            remote(sums_b.at[c], landed_b.at[row, u], plane_send_b, plane_recv_b.at[row], plane_device(u, half)).start()

    def completed_by(c):
        touched = range(2 * c * rows // channels, (2 * (c + 1) * rows - 1) // channels + 1)
        return max(i for i, group in enumerate(TAP_GROUPS) if any(t in group for t in touched))

    def each_chunk(chunks, body):
        def mirrored(c):
            body(c)
            body(n - 1 - c)

        starts = [c for c in chunks if c - 1 not in chunks]
        ends = [c + 1 for c in chunks if c + 1 not in chunks]
        for low, high in zip(starts, ends):
            loop(low, high, mirrored)

    completed = [[c for c in range(n // 2) if completed_by(c) == i] for i in range(len(TAP_GROUPS))]

    def pass_group(i):
        wait_all(theirs_b.at[pl.ds(0, 2 * len(completed[i]))], swap_recv_b.at[i])
        each_chunk(completed[i], pass_b)

    for i, group in enumerate(TAP_GROUPS):
        field_grad(group)
        each_chunk(completed[i], functools.partial(ready, i))
        if i:
            pass_group(i - 1)
    pass_group(len(TAP_GROUPS) - 1)

    def along_rows(k):
        row = jnp.where(side == 0, k, lines - 1 - k)
        wait_all(landed_b.at[row], plane_recv_b.at[row])
        total = lax.fori_loop(0, m - 1, lambda u, sofar: sofar + landed_b[row, u].astype(full), kept_b[row])
        kept_b[row] = total

        @pl.when(row != place.row)
        def _():
            t = lax.rem(row - place.row - 1 + lines, lines)
            passed_b[t] = total.astype(half_type)
            device = place.device(place.chip(place.plane, row), half)
            remote(passed_b.at[t], reached_b.at[t], row_send_b, row_recv_b, device).start()

    loop(0, lines, along_rows)
    wait_all(theirs, swap_send)
    wait_all(sums, plane_send)
    wait_all(squares, sq_send)
    wait_all(whole_other, relay_send)
    wait_all(params_own.at[pl.ds(0, lines - 1), 0], pass_send)
    wait_all(params_own.at[:, pl.ds(0, m - 1)], params_send)
    wait_all(params_own, carry_send)
    wait_all(whole_own.at[:, pl.ds(0, m - 1)], gather_send)
    for copy, out_of, into in halos:
        pl.when(out_of)(copy.wait_send)
    if place.doublings:
        wait_all(line_out, line_send)
    wait_all(theirs_b, swap_send_b)
    wait_all(sums_b.at[pl.ds(0, n - lines)], plane_send_b)
    wait_all(reached_b, row_recv_b)
    out[...] = lax.fori_loop(0, lines - 1, lambda t, sofar: sofar + reached_b[t].astype(full), kept_b[place.row])
    wait_all(reached_b, row_send_b)


def on_device(sizes, scenes, cotangent, params, partials):
    scenes, cotangent = scenes[0], cotangent[0]
    height, width, channels = scenes.shape
    n = sizes[0] * sizes[1] * sizes[2] // 2
    rows = params.size // LANES
    dma = pltpu.SemaphoreType.DMA
    half_type, full = jnp.bfloat16, jnp.float32
    anywhere, vmem = pl.BlockSpec(memory_space=pl.ANY), pl.BlockSpec(memory_space=pltpu.VMEM)
    lines, m = sizes[1], n // sizes[1]
    one = (rows, LANES)
    doublings = max((lines - 1).bit_length(), 1)
    scratch = [
        pltpu.VMEM(scenes.shape, half_type),
        pltpu.VMEM(scenes.shape, half_type),
        pltpu.VMEM((4, 2, width, channels), half_type),
        pltpu.VMEM((len(AROUND), 2, width, channels), half_type),
        pltpu.VMEM((2, height + 2, width, 3 * channels), half_type),
        pltpu.VMEM((2, height, channels), full),
        pltpu.VMEM((18 * channels, channels), full),
        pltpu.VMEM((2, 12 * channels, 2 * channels), half_type),
        pltpu.VMEM((height, width, channels), full),
        pltpu.VMEM((2, channels, height * width), half_type),
        pltpu.VMEM((n, 2, *one), full),
        pltpu.VMEM((sizes[0], lines, sizes[2] // 2, *one), full),
        pltpu.VMEM((1, 1, LANES), full),
        pltpu.VMEM((2 * m - 1, 1, LANES), full),
        pltpu.VMEM((lines, sizes[0], sizes[2] // 2, *one), full),
        pltpu.VMEM((n - lines, *one), half_type),
        pltpu.VMEM((lines, m - 1, *one), half_type),
        pltpu.VMEM((lines, *one), full),
        pltpu.VMEM((lines, *one), full),
        pltpu.VMEM((doublings, lines, *one), half_type),
        pltpu.VMEM((doublings, lines, *one), half_type),
        pltpu.VMEM((lines, m, *one), half_type),
        pltpu.VMEM((lines, m, *one), half_type),
        pltpu.VMEM((lines, m, *one), full),
        pltpu.VMEM((lines, m, *one), full),
        pltpu.VMEM((n, *one), full),
        pltpu.VMEM((n, *one), half_type),
        pltpu.VMEM((lines, m - 1, *one), half_type),
        pltpu.VMEM((lines, *one), full),
        pltpu.VMEM((lines - 1, *one), half_type),
        pltpu.VMEM((lines - 1, *one), half_type),
        dma((4,)), dma((len(AROUND),)), dma((len(AROUND),)),
        dma, dma((lines,)), dma, dma((lines,)), dma, dma((doublings, lines)),
        dma, dma, dma, dma((lines, m - 1)), dma, dma((2,)),
        dma, dma((doublings,)), dma, dma((2,)), dma, dma((2,)),
        dma, dma((len(TAP_GROUPS),)), dma, dma((lines,)), dma, dma,
    ]
    grads = pl.pallas_call(
        functools.partial(kernel, sizes, 32),
        out_shape=pltpu.VMEM((rows, LANES), full),
        in_specs=[anywhere, anywhere, anywhere, anywhere],
        out_specs=vmem,
        scratch_shapes=scratch,
        compiler_params=pltpu.CompilerParams(
            collective_id=0, has_side_effects=True, vmem_limit_bytes=56 * 2**20
        ),
        name="sam_grad",
    )(partials[0].reshape(sizes[0], lines, sizes[2] // 2, 2, rows, LANES), params.reshape(rows, LANES), scenes, cotangent)
    return grads.reshape(-1)


def solution(mesh):
    sizes = tuple(mesh.shape[axis] for axis in AXES)
    return jax.shard_map(
        functools.partial(on_device, sizes),
        mesh=mesh,
        in_specs=(
            P("scene", "row", "col", None),
            P("scene", "row", "col", None),
            P(AXES),
            P(AXES, None),
        ),
        out_specs=P(AXES),
        check_vma=False,
    )
```
